128 devices in a mesh: cells: 128 (over z, x, y, core).
Axes of the slice: x: 4, y: 4, z: 4, core: 2. Of those that a mesh axis runs over, the one named last changes fastest.
Arguments:
- channels: float32 [256, 41, 64, 128], P('cells'), may hold values from -0.44194174 to 0.44194174, as said below
- precoders_init: float32 [256, 16, 128], P('cells'), may hold values from -1 to 1
- receiver_cells: int32 [256], replicated, may hold values from 0 to 255, as said below
- transmitter_cells: int32 [256], replicated, may hold values from 0 to 255, as said below
- interferers: int32 [256, 40], replicated, may hold values from 0 to 255, as said below
- counts: int32 [256], replicated, may hold values from 24 to 40
Outputs:
- precoders: float32 [256, 16, 128], P('cells')
- mse_weights: float32 [256, 256], P('cells')
The draws below stay inside these ranges and needn't reach their ends.
Inputs may be any that keep to these rules, and one draw needn't show every extreme that they name: `receiver_cells`: A permutation of the cells; receiver slots s lie on device s // 2. `transmitter_cells`: A permutation of the cells; transmitter slots t lie on device t // 2. `interferers`: each row holds distinct cells, never the cell of its own receiver slot. Over the receiver slots of one device, the links in use (own links included) whose transmitter slot lies on any one device number at most 1, and 1 is reached in every draw. `channels`: own links (m = 0) are drawn stronger than interfering ones.
All inputs are finite; a program needn't handle non-finite values.
Results may differ from the reference program's by a relative error of at most 0.0003.
Values sent between devices are 32-bit elements; how exact they have to be, the bound alone decides.
A program may use at most 64 MiB of HBM per device.

```python
import jax
import jax.numpy as jnp
from jax import lax

NT = 128
NR = 64
D = 16
LMAX = 40
LMIN = 24
LAYERS = 4
CELL_DEV = 2
K = 256


def routing_tables(key):
    base_key = jax.random.fold_in(key, 4217)
    subkeys = jax.random.split(base_key, 5)
    devices = K // CELL_DEV
    link_count = LMAX + 1
    receivers = jax.random.permutation(subkeys[0], K).astype(jnp.int32)
    offsets = jax.random.permutation(subkeys[1], devices).astype(jnp.int32)
    member = jnp.arange(CELL_DEV, dtype=jnp.int32)
    own_device = (offsets[:, None] + link_count * member[None, :]) % devices
    senders = jnp.zeros((K,), jnp.int32).at[(own_device * CELL_DEV + member[None, :]).reshape(-1)].set(receivers)
    reaches = jnp.arange(1, link_count, dtype=jnp.int32)
    spread = member[:, None] * link_count + reaches[None, :]
    target_device = (offsets[:, None, None] + spread[None, :, :]) % devices
    jitter = jax.random.randint(subkeys[2], (devices, CELL_DEV, LMAX), 1, CELL_DEV).astype(jnp.int32)
    rotation = jnp.where((reaches % devices == 0)[None, None, :], 0, jitter)
    target_local = (member[None, :, None] + rotation + (reaches // devices)[None, None, :]) % CELL_DEV
    listing = senders[target_device * CELL_DEV + target_local].reshape(K, LMAX)
    full_device = jax.random.randint(subkeys[3], (), 0, devices)
    drawn_counts = jax.random.randint(subkeys[4], (K,), LMIN, LMAX + 1)
    counts = jnp.where(jnp.arange(K) // CELL_DEV == full_device, LMAX, drawn_counts).astype(jnp.int32)
    return (receivers, senders, listing, counts)


def draw_receiver_cells(key, part):
    return routing_tables(key)[0]


def draw_transmitter_cells(key, part):
    return routing_tables(key)[1]


def draw_interferers(key, part):
    return routing_tables(key)[2]


def draw_counts(key, part):
    return routing_tables(key)[3]


def draw_channels(key, part):
    subkeys = jax.random.split(jax.random.fold_in(key, 913), 2)
    shape = (K, LMAX + 1, NR, NT)
    entries = jnp.clip(jax.random.normal(subkeys[0], shape, jnp.float32), -5.0, 5.0)
    gains = jnp.exp(jax.random.uniform(subkeys[1], (K, LMAX + 1), jnp.float32, jnp.log(0.1), jnp.log(0.6)))
    gains = gains.at[:, 0].set(1.0)
    return entries * gains[:, :, None, None] * NT ** (-0.5)


def block_scale(stream_key, extent, pieces, smallest, high):
    def one(position, parts):
        draws = jax.random.uniform(jax.random.fold_in(jax.random.fold_in(stream_key, 6), position), (parts,), jnp.float32, smallest / len(pieces), high / len(pieces))
        return jnp.repeat(jnp.exp(draws), extent[position] // parts).reshape((-1,) + (1,) * (len(extent) - position - 1))

    gain = one(*pieces[0])
    for cut in pieces[1:]:
        gain = gain * one(*cut)
    return gain


def centred(rng, dims, scale, reach, pieces=(), kind=jnp.bfloat16):
    loudness = block_scale(rng, dims, pieces, -0.22, 0.18) if pieces else 1.0
    values = jax.random.normal(rng, dims, jnp.float32) * scale * loudness
    return jnp.minimum(jnp.maximum(values, -reach), reach).astype(kind)


def setup_inputs(seed: int = 0) -> dict:
    key_list = jax.random.split(jax.random.key(seed), 7)
    channels = draw_channels(jax.random.fold_in(key_list[6], 71), 0)
    precoders_init = centred(key_list[1], (K, D, NT), 0.25, 1.0, ((0, 128),), jnp.float32)
    receiver_cells = draw_receiver_cells(jax.random.fold_in(key_list[6], 71), 0)
    transmitter_cells = draw_transmitter_cells(jax.random.fold_in(key_list[6], 71), 0)
    interferers = draw_interferers(jax.random.fold_in(key_list[6], 71), 0)
    counts = draw_counts(jax.random.fold_in(key_list[6], 71), 0)
    return dict(channels=channels, precoders_init=precoders_init, receiver_cells=receiver_cells, transmitter_cells=transmitter_cells, interferers=interferers, counts=counts)


NOISE_POWER = 1.0
STEP_SIZES = (0.3, 0.2, 0.15, 0.1)
HIGHEST = lax.Precision.HIGHEST

def spd_solve(matrix, right_side):
    factor = jnp.linalg.cholesky(matrix)
    middle = lax.linalg.triangular_solve(factor, right_side, left_side=True, lower=True)
    return lax.linalg.triangular_solve(factor, middle, left_side=True, lower=True, transpose_a=True)

def link_tables(receiver_cells, transmitter_cells, interferers, counts):
    inverse = jnp.argsort(transmitter_cells).astype(jnp.int32)
    linked = jnp.concatenate([receiver_cells[:, None], interferers], axis=1)
    positions = inverse[linked]
    in_use = jnp.arange(interferers.shape[1] + 1, dtype=jnp.int32)[None, :] <= counts[:, None]
    return (positions, in_use)

def receiver_step(channels, link_precoders, in_use):
    weight_mask = in_use.astype(jnp.float32)
    images = jnp.einsum('klrn,kldn->kldr', channels, link_precoders, precision=HIGHEST)
    masked = images * weight_mask[:, :, None, None]
    receive_size = channels.shape[2]
    stream_count = link_precoders.shape[2]
    covariance = jnp.einsum('kldr,klds->krs', masked, images, precision=HIGHEST) + NOISE_POWER * jnp.eye(receive_size, dtype=jnp.float32)
    direct = images[:, 0]
    filters = spd_solve(covariance, jnp.swapaxes(direct, 1, 2))
    identity = jnp.eye(stream_count, dtype=jnp.float32)
    errors = identity - jnp.einsum('krd,ker->kde', filters, direct, precision=HIGHEST)
    weights = spd_solve(errors, jnp.broadcast_to(identity, errors.shape))
    transposed = jnp.einsum('krd,klrn->kldn', filters, channels, precision=HIGHEST) * weight_mask[:, :, None, None]
    return (weights, transposed)

def reference(channels, precoders_init, receiver_cells, transmitter_cells, interferers, counts):
    positions, in_use = link_tables(receiver_cells, transmitter_cells, interferers, counts)
    stream_count = precoders_init.shape[1]
    antenna_count = precoders_init.shape[2]
    precoders = precoders_init
    weights = jnp.zeros((K, stream_count, stream_count), jnp.float32)

    def accumulate(running, piece):
        filter_rows, weighted_rows, targets = piece
        products = jnp.einsum('ldn,ldm->lnm', filter_rows, weighted_rows, precision=HIGHEST)
        return (running.at[targets].add(products), None)
    for layer_index in range(LAYERS):
        link_precoders = precoders[positions]
        weights, transposed = receiver_step(channels, link_precoders, in_use)
        weighted = jnp.einsum('ked,klen->kldn', weights, transposed, precision=HIGHEST)
        start = jnp.zeros((K, antenna_count, antenna_count), jnp.float32)
        system, unused = lax.scan(accumulate, start, (transposed, weighted, positions))
        system = system + STEP_SIZES[layer_index] * jnp.eye(antenna_count, dtype=jnp.float32)
        right_side = jnp.zeros((K, stream_count, antenna_count), jnp.float32).at[positions[:, 0]].set(weighted[:, 0])
        precoders = jnp.swapaxes(spd_solve(system, jnp.swapaxes(right_side, 1, 2)), 1, 2)
    return (precoders, weights.reshape(K, stream_count * stream_count))
```

```python
import functools

import jax
import jax.numpy as jnp
from jax import lax
from jax.experimental import pallas as pl
from jax.experimental.pallas import tpu as pltpu
from jax.sharding import PartitionSpec as P

LAYERS = 4
STEP_SIZES = (0.3, 0.2, 0.15, 0.1)
HIGHEST = lax.Precision.HIGHEST
MESH = pl.DeviceIdType.MESH
F32, BF16 = jnp.float32, jnp.bfloat16
DEV = 128
GROUP = 16
GROUPS = DEV // GROUP
BLOCK = 8
NN = (((1,), (0,)), ((), ()))
NT = (((1,), (1,)), ((), ()))
TN = (((0,), (0,)), ((), ()))


def split(x):
    high = x.astype(BF16)
    return high, (x - high.astype(F32)).astype(BF16)


def mm(a, b, dims):
    return lax.dot_general(a, b, dims, preferred_element_type=F32)


def mm_exact(a, b, dims):
    return lax.dot_general(a, b, dims, precision=HIGHEST, preferred_element_type=F32)


def lanes():
    return lax.broadcasted_iota(jnp.int32, (8, 128), 1)


def pick_row(v, row):
    return jnp.broadcast_to(v[row : row + 1, :], (8, 128))


def pick_lane(v, k):
    return jnp.where(
        lanes() < 64,
        jnp.broadcast_to(v[:, k : k + 1], (8, 128)),
        jnp.broadcast_to(v[:, 64 + k : 65 + k], (8, 128)),
    )


def rows_of(x):
    return [x[8 * i : 8 * i + 8, :] for i in range(x.shape[0] // 8)]


def right_divide(rows):
    rows = list(rows)
    count = len(rows)
    spot = lanes() % 64
    for first in range(0, 64, BLOCK):
        top = first // 8
        columns = [{i: pick_lane(rows[i], first + j) for i in range(top, count)} for j in range(BLOCK)]
        pivots = [pick_row(rows[top], j) for j in range(BLOCK)]
        scaled = []
        for j in range(BLOCK):
            inverse = 1.0 / pick_row(columns[j][top], j)
            row = (pivots[j] - (spot == first + j).astype(F32)) * inverse
            scaled.append(row)
            for later in range(j + 1, BLOCK):
                factor = pick_row(columns[later][top], j) * inverse
                for i in range(top, count):
                    columns[later][i] = columns[later][i] - columns[j][i] * factor
                pivots[later] = pivots[later] - pick_row(columns[j][top], later) * row
        for i in range(top, count):
            total = rows[i]
            for j in range(BLOCK):
                total = total - columns[j][i] * scaled[j]
            rows[i] = total
    return rows[8:]


def lower_divide(w, v):
    ws, vs = rows_of(w), rows_of(v)
    line = lax.broadcasted_iota(jnp.int32, (8, 128), 0)
    diagonal = [jnp.ones((8, 128), F32), jnp.ones((8, 128), F32)]
    for k in range(16):
        top, at = divmod(k, 8)
        columns = {i: pick_lane(ws[i], k) for i in range(top, 2)}
        pivot = pick_row(columns[top], at)
        inverse = 1.0 / pivot
        wrow, vrow = pick_row(ws[top], at) * inverse, pick_row(vs[top], at) * inverse
        diagonal[top] = jnp.where(line == at, pivot, diagonal[top])
        for i in range(top, 2):
            column = jnp.where(line > at, columns[i], 0.0) if i == top else columns[i]
            ws[i] = ws[i] - column * wrow
            vs[i] = vs[i] - column * vrow
    out_l, out_v = [], []
    for i in range(2):
        scale = 1.0 / jnp.sqrt(diagonal[i])
        keep = (lanes() % 64 >= line + 8 * i) & (lanes() % 64 < 16)
        out_l.append(jnp.where(keep, ws[i] * scale, 0.0))
        out_v.append(vs[i] * scale)
    return out_l, jnp.concatenate(out_v, axis=0)


def kernel(
    tab, channels, first_precoders, precoders_out, weights_out,
    raw, links, current, psend, parr, gbuf, fsend, farr, lsend, larr, pair, acc1, acc2,
    raw_sem, psend_sem, precv, fsend_sem, frecv, lsend_sem, lrecv,
):
    me = lax.axis_index("cells")
    mz, mx, my, mc = me // 32, (me // 8) % 4, (me // 2) % 4, me % 2

    def target(i):
        dz, dx, dy, dc = i // 32, (i // 8) % 4, (i // 2) % 4, i % 2
        return (((mz + dz) % 4 * 4 + (mx + dx) % 4) * 4 + (my + dy) % 4) * 2 + (mc + dc) % 2

    def source(i):
        dz, dx, dy, dc = i // 32, (i // 8) % 4, (i // 2) % 4, i % 2
        return (((mz + 4 - dz) % 4 * 4 + (mx + 4 - dx) % 4) * 4 + (my + 4 - dy) % 4) * 2 + (mc + 2 - dc) % 2

    def step_from(d):
        z, x, y, c = d // 32, (d // 8) % 4, (d // 2) % 4, d % 2
        return (((mz + 4 - z) % 4 * 4 + (mx + 4 - x) % 4) * 4 + (my + 4 - y) % 4) * 2 + (mc + 2 - c) % 2

    def copy(src, dst, i, send, recv):
        return pltpu.make_async_remote_copy(
            src_ref=src, dst_ref=dst, send_sem=send, recv_sem=recv,
            device_id=(target(i),), device_id_type=MESH,
        )

    def wait_group(buf, g, send, recv, first):
        @pl.when(g == 0)
        def _():
            part = buf.at[pl.ds(1, GROUP - 1)]
            copy(part, part, 1, send, recv.at[0]).wait_recv()

        @pl.when(g > 0)
        def _():
            part = buf.at[pl.ds(g * GROUP, GROUP)]
            copy(part, part, 1, send, recv.at[g]).wait_recv()

    fetch = pltpu.make_async_copy(channels, raw, raw_sem)
    fetch.start()
    barrier = pltpu.get_barrier_semaphore()

    def greet(i, carry):
        pl.semaphore_signal(barrier, inc=1, device_id=(target(i),), device_id_type=MESH)
        return carry

    lax.fori_loop(1, DEV, greet, 0)
    current[...] = first_precoders[...]
    half = lax.broadcasted_iota(jnp.int32, (16, 128), 1) < 64
    left = lax.broadcasted_iota(jnp.int32, (64, 128), 1) < 64
    pl.semaphore_wait(barrier, DEV - 1)
    fetch.wait()

    def prepare(i, carry):
        high, low = split(raw[i])
        links[i, 0:64, :] = high
        links[i, 64:128, :] = low
        return carry

    def layer(index, carry):
        def select(i, carry):
            psend[i] = current[tab[4, target(i)]]
            return carry

        lax.fori_loop(0, DEV, select, 0, unroll=8)
        parr[0] = psend[0]

        def send_precoder(i, carry):
            copy(psend.at[i], parr.at[i], i, psend_sem, precv.at[i // GROUP]).start()
            return carry

        lax.fori_loop(1, DEV, send_precoder, 0)

        @pl.when(index == 0)
        def _():
            lax.fori_loop(0, 82, prepare, 0)

        acc1[...] = jnp.zeros((128, 256), F32)
        acc2[...] = jnp.zeros((128, 256), F32)

        def images(g, carry):
            wait_group(parr, g, psend_sem, precv, 1)
            highs, lows = [], []
            for j in range(GROUP):
                i = g * GROUP + j
                d = source(i)
                high, low = split(parr[i])
                product = mm(jnp.concatenate([high, low], axis=0), links[tab[0, d]], NT)
                total = product[0:16] + product[16:32]
                total = total + pltpu.roll(total, 64, 1)
                gbuf[i] = total
                masked = total * jnp.where(half, tab[1, d].astype(F32), tab[2, d].astype(F32))
                high, low = split(masked)
                highs.append(high)
                lows.append(low)
            high, low = jnp.concatenate(highs, axis=0), jnp.concatenate(lows, axis=0)
            acc1[:, 0:128] += mm(high, high, TN)
            acc2[:, 0:128] += mm(high, low, TN)
            return carry

        lax.fori_loop(0, GROUPS, images, 0)
        cross = acc2[:, 0:128]
        full = acc1[:, 0:128] + cross + cross.T
        line = lax.broadcasted_iota(jnp.int32, (64, 128), 0)
        spot = lax.broadcasted_iota(jnp.int32, (64, 128), 1) % 64
        covariance = jnp.where(left, full[0:64], full[64:128]) + (line == spot).astype(F32)
        direct = jnp.where(half, gbuf[step_from(tab[5, 0])], gbuf[step_from(tab[5, 1])])
        v = jnp.concatenate(right_divide(rows_of(covariance) + rows_of(direct))[0:2], axis=0)
        blank = jnp.zeros((48, 128), F32)
        apart = jnp.concatenate(
            [jnp.where(half, direct, 0.0), blank, jnp.where(half, 0.0, direct), blank], axis=0
        )
        short = lax.broadcasted_iota(jnp.int32, (16, 128), 0)
        w = mm_exact(v, apart, NT)
        w = w + (lax.broadcasted_iota(jnp.int32, (16, 128), 1) % 64 == short).astype(F32)
        weights_out[...] = w
        lower, filters = lower_divide(w, v)
        for s in range(2):
            mine = jnp.where(half, filters, 0.0) if s == 0 else jnp.where(half, 0.0, filters)
            mine = mine + pltpu.roll(mine, 64, 1)
            high, low = split(mine)
            pair[s] = jnp.concatenate([high, low], axis=0)
        packed = lower[0] + pltpu.roll(lower[1], 16, 1)

        def filter_group(g, carry):
            for j in range(GROUP):
                i = g * GROUP + j
                at = tab[0, target(i)]
                product = mm(pair[at // 41], links[at], NN)
                fsend[i] = product[0:16] + product[16:32]

            def send_filter(i, carry):
                copy(fsend.at[i], farr.at[i], i, fsend_sem, frecv.at[i // GROUP]).start()
                return carry

            lax.fori_loop(jnp.where(g == 0, 1, g * GROUP), (g + 1) * GROUP, send_filter, 0)
            return carry

        lax.fori_loop(0, GROUPS, filter_group, 0)
        farr[0] = fsend[0]
        lsend[...] = packed
        larr[0] = packed
        acc1[...] = jnp.zeros((128, 256), F32)
        acc2[...] = jnp.zeros((128, 256), F32)

        def send_lower(i, carry):
            copy(lsend, larr.at[i], i, lsend_sem, lrecv).start()
            return carry

        lax.fori_loop(1, DEV, send_lower, 0)

        def gather_group(g, carry):
            wait_group(farr, g, fsend_sem, frecv, 1)
            highs, lows, highs01, lows01 = [], [], [], []
            for j in range(GROUP):
                i = g * GROUP + j
                d = source(i)
                m0, m1 = tab[3, d].astype(F32), tab[4, d].astype(F32)
                f = farr[i]
                highs.append(f.astype(BF16))
                high, low = split(jnp.concatenate([f * m0, f * m1], axis=1))
                highs01.append(high)
                lows01.append(low)
            high = jnp.concatenate(highs, axis=0)
            acc1[...] += mm(high, jnp.concatenate(highs01, axis=0), TN)
            acc2[...] += mm(high, jnp.concatenate(lows01, axis=0), TN)
            return carry

        lax.fori_loop(0, GROUPS, gather_group, 0)
        mu = jnp.where(index == 0, STEP_SIZES[0], jnp.where(index == 1, STEP_SIZES[1], jnp.where(index == 2, STEP_SIZES[2], STEP_SIZES[3]))).astype(F32)
        eye = (
            lax.broadcasted_iota(jnp.int32, (128, 128), 0) == lax.broadcasted_iota(jnp.int32, (128, 128), 1)
        ).astype(F32) * mu
        systems = []
        for t in range(2):
            cross = acc2[:, 128 * t : 128 * t + 128]
            systems.append(acc1[:, 128 * t : 128 * t + 128] + cross + cross.T + eye)
        a0, a1 = systems
        steps = [step_from(tab[5, 2 + t] // 2) for t in range(2)]
        b0, b1 = farr[steps[0]], farr[steps[1]]
        upper = jnp.where(left, a0[0:64], a1[64:128])
        under = jnp.where(left, a0[64:128], a1[0:64])
        solved = right_divide(rows_of(upper) + rows_of(under) + rows_of(jnp.where(half, b0, b1)))
        solved = jnp.concatenate(solved, axis=0)
        beside = jnp.concatenate([jnp.where(left, 0.0, a0[0:64]), jnp.where(left, a1[64:128], 0.0)], axis=0)
        update = mm_exact(solved, beside, NN)
        rest = jnp.where(left, a1[0:64], a0[64:128]) - update[0:64]
        side = jnp.where(half, b1, b0) - update[64:80]
        second = jnp.concatenate(right_divide(rows_of(rest) + rows_of(side))[0:2], axis=0)
        under = solved[0:64]
        back = jnp.concatenate([jnp.where(left, 0.0, under), jnp.where(left, under, 0.0)], axis=0)
        first = solved[64:80] - mm_exact(second, back, NN)
        answers = [jnp.where(half, first, second), jnp.where(half, second, first)]

        copies = copy(larr.at[pl.ds(1, DEV - 1)], larr.at[pl.ds(1, DEV - 1)], 1, lsend_sem, lrecv)
        copies.wait_recv()
        copies.wait_send()
        everyone = pl.ds(1, DEV - 1)
        copy(psend.at[everyone], parr.at[everyone], 1, psend_sem, precv.at[0]).wait_send()
        copy(fsend.at[everyone], farr.at[everyone], 1, fsend_sem, frecv.at[0]).wait_send()
        low16 = lanes() < 16
        for t in range(2):
            got = larr[steps[t]]
            got = jnp.where(tab[5, 2 + t] % 2 == 0, got, pltpu.roll(got, 64, 1))
            triangle = jnp.concatenate(
                [jnp.where(low16, got, 0.0), jnp.where(low16, pltpu.roll(got, 112, 1), 0.0)], axis=0
            )
            current[t] = mm_exact(triangle, answers[t], TN)[0:16]
        return carry

    lax.fori_loop(0, LAYERS, layer, 0)
    precoders_out[...] = current[...]


def tables(receiver_cells, transmitter_cells, interferers, counts):
    me = lax.axis_index("cells")
    linked = jnp.concatenate([receiver_cells[:, None], interferers], axis=1)
    in_use = jnp.arange(41, dtype=jnp.int32)[None, :] <= counts[:, None]
    mine = lax.dynamic_slice(linked, (2 * me, 0), (2, 41)).reshape(82)
    mine_use = lax.dynamic_slice(in_use, (2 * me, 0), (2, 41)).reshape(82)
    match = mine_use[:, None, None] & (mine[:, None, None] == transmitter_cells.reshape(1, DEV, 2))
    match = jnp.any(match, axis=2)
    number = jnp.arange(82, dtype=jnp.int32)[:, None]
    link = jnp.sum(jnp.where(match, number, 0), axis=0)
    apart = match & (number % 41 > 0)
    own0 = jnp.sum((apart & (number < 41)).astype(jnp.int32), axis=0)
    own1 = jnp.sum((apart & (number >= 41)).astype(jnp.int32), axis=0)
    cells = lax.dynamic_slice(transmitter_cells, (2 * me,), (2,))
    wanted = in_use[:, :, None] & (linked[:, :, None] == cells[None, None, :])
    wanted = jnp.any(jnp.any(wanted, axis=1).reshape(DEV, 2, 2), axis=1).astype(jnp.int32)
    place = jnp.arange(256, dtype=jnp.int32)
    heads = lax.dynamic_slice(receiver_cells, (2 * me,), (2,))
    from_device = jnp.sum(jnp.where(transmitter_cells[None, :] == heads[:, None], place[None, :] // 2, 0), axis=1)
    served = jnp.sum(jnp.where(receiver_cells[None, :] == cells[:, None], place[None, :], 0), axis=1)
    misc = jnp.concatenate([from_device, served, jnp.zeros((DEV - 4,), jnp.int32)])
    return jnp.stack([link, own0, own1, wanted[:, 0], wanted[:, 1], misc])


def body(channels, precoders_init, receiver_cells, transmitter_cells, interferers, counts):
    tab = tables(receiver_cells, transmitter_cells, interferers, counts)
    dma = pltpu.SemaphoreType.DMA
    precoders, weights = pl.pallas_call(
        kernel,
        out_shape=(
            jax.ShapeDtypeStruct((2, 16, 128), F32),
            jax.ShapeDtypeStruct((16, 128), F32),
        ),
        in_specs=[
            pl.BlockSpec(memory_space=pltpu.SMEM),
            pl.BlockSpec(memory_space=pl.ANY),
            pl.BlockSpec(memory_space=pltpu.VMEM),
        ],
        out_specs=(pl.BlockSpec(memory_space=pltpu.VMEM), pl.BlockSpec(memory_space=pltpu.VMEM)),
        scratch_shapes=[
            pltpu.VMEM((82, 64, 128), F32),
            pltpu.VMEM((82, 128, 128), BF16),
            pltpu.VMEM((2, 16, 128), F32),
            pltpu.VMEM((DEV, 16, 128), F32),
            pltpu.VMEM((DEV, 16, 128), F32),
            pltpu.VMEM((DEV, 16, 128), F32),
            pltpu.VMEM((DEV, 16, 128), F32),
            pltpu.VMEM((DEV, 16, 128), F32),
            pltpu.VMEM((8, 128), F32),
            pltpu.VMEM((DEV, 8, 128), F32),
            pltpu.VMEM((2, 32, 128), BF16),
            pltpu.VMEM((128, 256), F32),
            pltpu.VMEM((128, 256), F32),
            dma, dma, dma((GROUPS,)), dma, dma((GROUPS,)), dma, dma,
        ],
        compiler_params=pltpu.CompilerParams(collective_id=0, has_side_effects=True),
    )(tab, channels.reshape(82, 64, 128), precoders_init)
    weights = jnp.stack([weights[:, 0:16], weights[:, 64:80]]).reshape(2, 256)
    return (precoders, weights)


def solution(mesh):
    return jax.shard_map(
        body,
        mesh=mesh,
        in_specs=(P("cells", None, None, None), P("cells", None, None), P(), P(), P(), P()),
        out_specs=(P("cells", None, None), P("cells", None)),
        check_vma=False,
    )
```

```python
import functools

import jax
import jax.numpy as jnp
from jax import lax
from jax.experimental import pallas as pl
from jax.experimental.pallas import tpu as pltpu
from jax.sharding import PartitionSpec as P

LAYERS = 4
STEP_SIZES = (0.3, 0.2, 0.15, 0.1)
HIGHEST = lax.Precision.HIGHEST
MESH = pl.DeviceIdType.MESH
F32, BF16 = jnp.float32, jnp.bfloat16
DEV = 128
GROUP = 16
GROUPS = DEV // GROUP
OFFSETS = sorted(
    ((z, x, y, c) for z in range(4) for x in range(4) for y in range(4) for c in range(2)),
    key=lambda o: -sum(min(a, 4 - a) for a in o[:3]) - 0.5 * o[3],
)
NUMBERS = [((z * 4 + x) * 4 + y) * 2 + c for z, x, y, c in OFFSETS]
NN = (((1,), (0,)), ((), ()))
NT = (((1,), (1,)), ((), ()))
TN = (((0,), (0,)), ((), ()))


def split(x):
    high = x.astype(BF16)
    return high, (x - high.astype(F32)).astype(BF16)


def mm(a, b, dims):
    return lax.dot_general(a, b, dims, preferred_element_type=F32)


def mm_exact(a, b, dims):
    return lax.dot_general(a, b, dims, precision=HIGHEST, preferred_element_type=F32)


def lanes():
    return lax.broadcasted_iota(jnp.int32, (8, 128), 1)


def pick_row(v, row):
    return jnp.broadcast_to(v[row : row + 1, :], (8, 128))


def pick_lane(v, k):
    return jnp.take_along_axis(v, jnp.where(lanes() < 64, k, 64 + k), axis=1)


def rows_of(x):
    return [x[8 * i : 8 * i + 8, :] for i in range(x.shape[0] // 8)]


def right_divide(rows):
    rows = list(rows)
    spot, line = lanes() % 64, lax.broadcasted_iota(jnp.int32, (8, 128), 0)
    for top in range(8):
        columns = [pick_lane(rows[top], 8 * top + j) for j in range(8)]
        x = rows[top] - (spot == line + 8 * top).astype(F32)
        for j in range(8):
            factor = (columns[j] - (line == j).astype(F32)) * (1.0 / pick_row(columns[j], j))
            for later in range(j + 1, 8):
                columns[later] = columns[later] - factor * pick_row(columns[later], j)
            x = x - factor * pick_row(x, j)
        pivots = [pick_row(x, j) for j in range(8)]
        for i in range(top + 1, len(rows)):
            total = rows[i]
            for j in range(8):
                total = total - pick_lane(rows[i], 8 * top + j) * pivots[j]
            rows[i] = total
    return rows[8:]


def lower_divide(w, v):
    ws, vs = rows_of(w), rows_of(v)
    line = lax.broadcasted_iota(jnp.int32, (8, 128), 0)
    diagonal = [jnp.ones((8, 128), F32), jnp.ones((8, 128), F32)]
    for top in range(2):
        columns = [[pick_lane(ws[i], 8 * top + j) for i in range(top, 2)] for j in range(8)]
        for j in range(8):
            pivot = pick_row(columns[j][0], j)
            inverse = 1.0 / pivot
            factors = [c * inverse for c in columns[j]]
            factors[0] = jnp.where(line > j, factors[0], 0.0)
            diagonal[top] = jnp.where(line == j, pivot, diagonal[top])
            for later in range(j + 1, 8):
                row = pick_row(columns[later][0], j)
                columns[later] = [c - f * row for c, f in zip(columns[later], factors)]
            wrow, vrow = pick_row(ws[top], j), pick_row(vs[top], j)
            for i in range(top, 2):
                ws[i] = ws[i] - factors[i - top] * wrow
                vs[i] = vs[i] - factors[i - top] * vrow
    out_l, out_v = [], []
    for i in range(2):
        scale = 1.0 / jnp.sqrt(diagonal[i])
        keep = (lanes() % 64 >= line + 8 * i) & (lanes() % 64 < 16)
        out_l.append(jnp.where(keep, ws[i] * scale, 0.0))
        out_v.append(vs[i] * scale)
    return out_l, jnp.concatenate(out_v, axis=0)


def kernel(
    tab, channels, first_precoders, precoders_out, weights_out,
    raw, links, current, psend, parr, gbuf, fsend, farr, lsend, larr, pair, acc1, acc2,
    raw_sem, psend_sem, precv, fsend_sem, frecv, lsend_sem, lrecv,
):
    me = lax.axis_index("cells")
    mz, mx, my, mc = me // 32, (me // 8) % 4, (me // 2) % 4, me % 2

    zs = [lax.rem(mz + a, 4) * 32 for a in range(4)]
    xs = [lax.rem(mx + a, 4) * 8 for a in range(4)]
    ys = [lax.rem(my + a, 4) * 2 for a in range(4)]
    cs = [mc, 1 - mc]

    def target(k):
        dz, dx, dy, dc = OFFSETS[k]
        return zs[dz] + xs[dx] + ys[dy] + cs[dc]

    def source(k):
        dz, dx, dy, dc = OFFSETS[k]
        return zs[(4 - dz) % 4] + xs[(4 - dx) % 4] + ys[(4 - dy) % 4] + cs[dc]

    def step_from(d):
        z, x, y, c = d // 32, (d // 8) % 4, (d // 2) % 4, d % 2
        number = (((mz + 4 - z) % 4 * 4 + (mx + 4 - x) % 4) * 4 + (my + 4 - y) % 4) * 2 + (mc + 2 - c) % 2
        return tab[6, number]

    def copy(src, dst, i, send, recv):
        return pltpu.make_async_remote_copy(
            src_ref=src, dst_ref=dst, send_sem=send, recv_sem=recv,
            device_id=(target(i),), device_id_type=MESH,
        )

    remote = pl.ds(0, DEV - 1)

    def wait_group(buf, g, send, recv):
        part = buf.at[pl.ds(g * GROUP, GROUP - 1 if g == GROUPS - 1 else GROUP)]
        copy(part, part, 0, send, recv.at[g]).wait_recv()

    fetch = pltpu.make_async_copy(channels, raw, raw_sem)
    fetch.start()
    barrier = pltpu.get_barrier_semaphore()

    for k in range(DEV - 1):
        pl.semaphore_signal(barrier, inc=1, device_id=(target(k),), device_id_type=MESH)
    current[...] = first_precoders[...]
    half = lax.broadcasted_iota(jnp.int32, (16, 128), 1) < 64
    left = lax.broadcasted_iota(jnp.int32, (64, 128), 1) < 64

    def prepare(i, carry):
        high, low = split(raw[i])
        links[i, 0:64, :] = high
        links[i, 64:128, :] = low
        return carry

    fetch.wait()
    lax.fori_loop(0, 82, prepare, 0)
    pl.semaphore_wait(barrier, DEV - 1)

    def layer(index, carry):
        for g in range(GROUPS):
            for k in range(g * GROUP, g * GROUP + GROUP):
                psend[k] = current[tab[4, target(k)]]
            for k in range(g * GROUP, min(g * GROUP + GROUP, DEV - 1)):
                copy(psend.at[k], parr.at[k], k, psend_sem, precv.at[g]).start()
        parr[DEV - 1] = psend[DEV - 1]

        acc1[...] = jnp.zeros((128, 256), F32)
        acc2[...] = jnp.zeros((128, 256), F32)

        for g in range(GROUPS):
            wait_group(parr, g, psend_sem, precv)
            highs, lows = [], []
            for i in range(g * GROUP, g * GROUP + GROUP):
                d = source(i)
                high, low = split(parr[i])
                product = mm(jnp.concatenate([high, low], axis=0), links[tab[0, d]], NT)
                total = product[0:16] + product[16:32]
                total = total + pltpu.roll(total, 64, 1)
                gbuf[i] = total
                masked = total * jnp.where(half, tab[1, d].astype(F32), tab[2, d].astype(F32))
                high, low = split(masked)
                highs.append(high)
                lows.append(low)
            high, low = jnp.concatenate(highs, axis=0), jnp.concatenate(lows, axis=0)
            acc1[:, 0:128] += mm(high, high, TN)
            acc2[:, 0:128] += mm(high, low, TN)

        cross = acc2[:, 0:128]
        full = acc1[:, 0:128] + cross + cross.T
        line = lax.broadcasted_iota(jnp.int32, (64, 128), 0)
        spot = lax.broadcasted_iota(jnp.int32, (64, 128), 1) % 64
        covariance = jnp.where(left, full[0:64], full[64:128]) + (line == spot).astype(F32)
        direct = jnp.where(half, gbuf[step_from(tab[5, 0])], gbuf[step_from(tab[5, 1])])
        v = jnp.concatenate(right_divide(rows_of(covariance) + rows_of(direct))[0:2], axis=0)
        blank = jnp.zeros((48, 128), F32)
        apart = jnp.concatenate(
            [jnp.where(half, direct, 0.0), blank, jnp.where(half, 0.0, direct), blank], axis=0
        )
        short = lax.broadcasted_iota(jnp.int32, (16, 128), 0)
        w = mm_exact(v, apart, NT)
        w = w + (lax.broadcasted_iota(jnp.int32, (16, 128), 1) % 64 == short).astype(F32)
        weights_out[...] = w
        lower, filters = lower_divide(w, v)
        for s in range(2):
            mine = jnp.where(half, filters, 0.0) if s == 0 else jnp.where(half, 0.0, filters)
            mine = mine + pltpu.roll(mine, 64, 1)
            high, low = split(mine)
            pair[s] = jnp.concatenate([high, low], axis=0)
        for s in range(2):
            for i in range(2):
                part = lower[i] if s == 0 else pltpu.roll(lower[i], 64, 1)
                part = pltpu.roll(jnp.where(lanes() < 16, part, 0.0), 0, 1, stride=16, stride_axis=0)
                lsend[2 * s + i : 2 * s + i + 1, :] = jnp.sum(part, axis=0, keepdims=True)
        larr[DEV - 1] = lsend[...]

        for g in range(GROUPS):
            for k in range(g * GROUP, g * GROUP + GROUP):
                d = target(k)
                product = mm(pair[tab[7, d]], links[tab[0, d]], NN)
                fsend[k] = product[0:16] + product[16:32]
            for k in range(g * GROUP, min(g * GROUP + GROUP, DEV - 1)):
                copy(fsend.at[k], farr.at[k], k, fsend_sem, frecv.at[g]).start()
        farr[DEV - 1] = fsend[DEV - 1]
        acc1[...] = jnp.zeros((128, 256), F32)
        acc2[...] = jnp.zeros((128, 256), F32)

        for k in range(DEV - 1):
            copy(lsend, larr.at[k], k, lsend_sem, lrecv).start()

        for g in range(GROUPS):
            wait_group(farr, g, fsend_sem, frecv)
            highs, lows, highs01, lows01 = [], [], [], []
            for i in range(g * GROUP, g * GROUP + GROUP):
                d = source(i)
                m0, m1 = tab[3, d].astype(F32), tab[4, d].astype(F32)
                f = farr[i]
                highs.append(f.astype(BF16))
                high, low = split(jnp.concatenate([f * m0, f * m1], axis=1))
                highs01.append(high)
                lows01.append(low)
            high = jnp.concatenate(highs, axis=0)
            acc1[...] += mm(high, jnp.concatenate(highs01, axis=0), TN)
            acc2[...] += mm(high, jnp.concatenate(lows01, axis=0), TN)

        mu = jnp.where(index == 0, STEP_SIZES[0], jnp.where(index == 1, STEP_SIZES[1], jnp.where(index == 2, STEP_SIZES[2], STEP_SIZES[3]))).astype(F32)
        eye = (
            lax.broadcasted_iota(jnp.int32, (128, 128), 0) == lax.broadcasted_iota(jnp.int32, (128, 128), 1)
        ).astype(F32) * mu
        systems = []
        for t in range(2):
            cross = acc2[:, 128 * t : 128 * t + 128]
            systems.append(acc1[:, 128 * t : 128 * t + 128] + cross + cross.T + eye)
        a0, a1 = systems
        steps = [step_from(tab[5, 2 + t] // 2) for t in range(2)]
        b0, b1 = farr[steps[0]], farr[steps[1]]
        upper = jnp.where(left, a0[0:64], a1[64:128])
        under = jnp.where(left, a0[64:128], a1[0:64])
        solved = right_divide(rows_of(upper) + rows_of(under) + rows_of(jnp.where(half, b0, b1)))
        solved = jnp.concatenate(solved, axis=0)
        beside = jnp.concatenate([jnp.where(left, 0.0, a0[0:64]), jnp.where(left, a1[64:128], 0.0)], axis=0)
        update = mm_exact(solved, beside, NN)
        rest = jnp.where(left, a1[0:64], a0[64:128]) - update[0:64]
        side = jnp.where(half, b1, b0) - update[64:80]
        second = jnp.concatenate(right_divide(rows_of(rest) + rows_of(side))[0:2], axis=0)
        under = solved[0:64]
        back = jnp.concatenate([jnp.where(left, 0.0, under), jnp.where(left, under, 0.0)], axis=0)
        first = solved[64:80] - mm_exact(second, back, NN)
        answers = [jnp.where(half, first, second), jnp.where(half, second, first)]

        lowers = copy(larr.at[remote], larr.at[remote], 0, lsend_sem, lrecv)
        lowers.wait_recv()
        lowers.wait_send()
        copy(psend.at[remote], parr.at[remote], 0, psend_sem, precv.at[0]).wait_send()
        copy(fsend.at[remote], farr.at[remote], 0, fsend_sem, frecv.at[0]).wait_send()
        low16 = lanes() < 16
        unpack = (lanes() + 16 * lax.broadcasted_iota(jnp.int32, (8, 128), 0)) % 128
        for t in range(2):
            got = larr[steps[t]]
            got = jnp.where(tab[5, 2 + t] % 2 == 0, got[0:2], got[2:4])
            triangle = jnp.concatenate(
                [
                    jnp.where(low16, jnp.take_along_axis(pick_row(got, i), unpack, axis=1), 0.0)
                    for i in range(2)
                ],
                axis=0,
            )
            current[t] = mm_exact(triangle, answers[t], TN)[0:16]
        return carry

    lax.fori_loop(0, LAYERS, layer, 0)
    precoders_out[...] = current[...]


def tables(receiver_cells, transmitter_cells, interferers, counts):
    me = lax.axis_index("cells")
    linked = jnp.concatenate([receiver_cells[:, None], interferers], axis=1)
    in_use = jnp.arange(41, dtype=jnp.int32)[None, :] <= counts[:, None]
    mine = lax.dynamic_slice(linked, (2 * me, 0), (2, 41)).reshape(82)
    mine_use = lax.dynamic_slice(in_use, (2 * me, 0), (2, 41)).reshape(82)
    match = mine_use[:, None, None] & (mine[:, None, None] == transmitter_cells.reshape(1, DEV, 2))
    match = jnp.any(match, axis=2)
    number = jnp.arange(82, dtype=jnp.int32)[:, None]
    link = jnp.sum(jnp.where(match, number, 0), axis=0)
    apart = match & (number % 41 > 0)
    own0 = jnp.sum((apart & (number < 41)).astype(jnp.int32), axis=0)
    own1 = jnp.sum((apart & (number >= 41)).astype(jnp.int32), axis=0)
    cells = lax.dynamic_slice(transmitter_cells, (2 * me,), (2,))
    wanted = in_use[:, :, None] & (linked[:, :, None] == cells[None, None, :])
    wanted = jnp.any(jnp.any(wanted, axis=1).reshape(DEV, 2, 2), axis=1).astype(jnp.int32)
    place = jnp.arange(256, dtype=jnp.int32)
    heads = lax.dynamic_slice(receiver_cells, (2 * me,), (2,))
    from_device = jnp.sum(jnp.where(transmitter_cells[None, :] == heads[:, None], place[None, :] // 2, 0), axis=1)
    served = jnp.sum(jnp.where(receiver_cells[None, :] == cells[:, None], place[None, :], 0), axis=1)
    misc = jnp.concatenate([from_device, served, jnp.zeros((DEV - 4,), jnp.int32)])
    order = jnp.asarray(NUMBERS, jnp.int32)
    position = jnp.sum(jnp.where(order[:, None] == jnp.arange(DEV)[None, :], jnp.arange(DEV)[:, None], 0), axis=0)
    second = jnp.any(match & (number >= 41), axis=0).astype(jnp.int32)
    return jnp.stack([link, own0, own1, wanted[:, 0], wanted[:, 1], misc, position, second])


def body(channels, precoders_init, receiver_cells, transmitter_cells, interferers, counts):
    tab = tables(receiver_cells, transmitter_cells, interferers, counts)
    dma = pltpu.SemaphoreType.DMA
    precoders, weights = pl.pallas_call(
        kernel,
        out_shape=(
            jax.ShapeDtypeStruct((2, 16, 128), F32),
            jax.ShapeDtypeStruct((16, 128), F32),
        ),
        in_specs=[
            pl.BlockSpec(memory_space=pltpu.SMEM),
            pl.BlockSpec(memory_space=pl.ANY),
            pl.BlockSpec(memory_space=pltpu.VMEM),
        ],
        out_specs=(pl.BlockSpec(memory_space=pltpu.VMEM), pl.BlockSpec(memory_space=pltpu.VMEM)),
        scratch_shapes=[
            pltpu.VMEM((82, 64, 128), F32),
            pltpu.VMEM((82, 128, 128), BF16),
            pltpu.VMEM((2, 16, 128), F32),
            pltpu.VMEM((DEV, 16, 128), F32),
            pltpu.VMEM((DEV, 16, 128), F32),
            pltpu.VMEM((DEV, 16, 128), F32),
            pltpu.VMEM((DEV, 16, 128), F32),
            pltpu.VMEM((DEV, 16, 128), F32),
            pltpu.VMEM((4, 128), F32),
            pltpu.VMEM((DEV, 4, 128), F32),
            pltpu.VMEM((2, 32, 128), BF16),
            pltpu.VMEM((128, 256), F32),
            pltpu.VMEM((128, 256), F32),
            dma, dma, dma((GROUPS,)), dma, dma((GROUPS,)), dma, dma,
        ],
        compiler_params=pltpu.CompilerParams(collective_id=0, has_side_effects=True),
    )(tab, channels.reshape(82, 64, 128), precoders_init)
    weights = jnp.stack([weights[:, 0:16], weights[:, 64:80]]).reshape(2, 256)
    return (precoders, weights)


def solution(mesh):
    return jax.shard_map(
        body,
        mesh=mesh,
        in_specs=(P("cells", None, None, None), P("cells", None, None), P(), P(), P(), P()),
        out_specs=(P("cells", None, None), P("cells", None)),
        check_vma=False,
    )
```

```python
import random

import jax
import jax.numpy as jnp
from jax import lax
from jax.experimental import pallas as pl
from jax.experimental.pallas import tpu as pltpu
from jax.sharding import PartitionSpec as P

LAYERS = 4
STEP_SIZES = (0.3, 0.2, 0.15, 0.1)
HIGHEST = lax.Precision.HIGHEST
MESH = pl.DeviceIdType.MESH
F32, BF16 = jnp.float32, jnp.bfloat16
DEV = 128
OFFSETS = [(z, x, y, c) for z in range(4) for x in range(4) for y in range(4) for c in range(2)]
shuffled = random.Random(5)
ORDER = sorted(range(DEV), key=lambda i: (-sum(min(a, 4 - a) for a in OFFSETS[i][:3]), -i if i < 2 else shuffled.random()))
SIZES = [8, 8, 16, 16, 16, 16, 16, 16, 8, 8]
GROUPS = [ORDER[sum(SIZES[:g]) : sum(SIZES[: g + 1])] for g in range(len(SIZES))]
LAST = len(GROUPS) - 1
LATE = 7
NN = (((1,), (0,)), ((), ()))
NT = (((1,), (1,)), ((), ()))
TN = (((0,), (0,)), ((), ()))


def split(x):
    high = x.astype(BF16)
    return high, (x - high.astype(F32)).astype(BF16)


def mm(a, b, dims):
    return lax.dot_general(a, b, dims, preferred_element_type=F32)


def mm_exact(a, b, dims):
    return lax.dot_general(a, b, dims, precision=HIGHEST, preferred_element_type=F32)


def mm_split(a, b, dims):
    (ah, al), (bh, bl) = split(a), split(b)
    return mm(ah, bh, dims) + (mm(ah, bl, dims) + mm(al, bh, dims))


def lanes():
    return lax.broadcasted_iota(jnp.int32, (8, 128), 1)


def pick_row(v, row):
    return jnp.broadcast_to(v[row : row + 1, :], (8, 128))


def pick_lane(v, k):
    return jnp.take_along_axis(v, jnp.where(lanes() < 64, k, 64 + k), axis=1)


def rows_of(x):
    return [x[8 * i : 8 * i + 8, :] for i in range(x.shape[0] // 8)]


def clear_block(rows, top, others):
    spot, line = lanes() % 64, lax.broadcasted_iota(jnp.int32, (8, 128), 0)
    columns = [pick_lane(rows[top], 8 * top + j) for j in range(8)]
    unit = (spot == line + 8 * top).astype(F32)
    x = rows[top] - unit
    for j in range(0, 8, 2):
        a, b = columns[j], columns[j + 1]
        p11, p21, p12, p22 = pick_row(a, j), pick_row(a, j + 1), pick_row(b, j), pick_row(b, j + 1)
        inverse = 1.0 / (p11 * p22 - p12 * p21)
        a, b = a - (line == j).astype(F32), b - (line == j + 1).astype(F32)
        one, two = (a * p22 - b * p21) * inverse, (b * p11 - a * p12) * inverse
        for later in range(j + 2, 8):
            column = columns[later]
            columns[later] = column - one * pick_row(column, j) - two * pick_row(column, j + 1)
        x = x - one * pick_row(x, j) - two * pick_row(x, j + 1)
    pivots = [pick_row(x, j) for j in range(8)]
    for i in others:
        t = [pick_lane(rows[i], 8 * top + j) * pivots[j] for j in range(8)]
        rows[i] = rows[i] - (((t[0] + t[1]) + (t[2] + t[3])) + ((t[4] + t[5]) + (t[6] + t[7])))
    rows[top] = unit - x


def right_divide(rows):
    rows = list(rows)
    for top in range(8):
        clear_block(rows, top, range(top + 1, len(rows)))
    return rows[8:]


def invert(rows):
    rows = list(rows)
    for top in range(8):
        clear_block(rows, top, [i for i in range(8) if i != top])
    return jnp.concatenate(rows, axis=0)


def lower_divide(w, v):
    ws, vs = rows_of(w), rows_of(v)
    line = lax.broadcasted_iota(jnp.int32, (8, 128), 0)
    diagonal = [jnp.ones((8, 128), F32), jnp.ones((8, 128), F32)]
    for top in range(2):
        columns = [[pick_lane(ws[i], 8 * top + j) for i in range(top, 2)] for j in range(8)]
        for j in range(8):
            pivot = pick_row(columns[j][0], j)
            inverse = 1.0 / pivot
            factors = [c * inverse for c in columns[j]]
            factors[0] = jnp.where(line > j, factors[0], 0.0)
            diagonal[top] = jnp.where(line == j, pivot, diagonal[top])
            for later in range(j + 1, 8):
                row = pick_row(columns[later][0], j)
                columns[later] = [c - f * row for c, f in zip(columns[later], factors)]
            wrow, vrow = pick_row(ws[top], j), pick_row(vs[top], j)
            for i in range(top, 2):
                ws[i] = ws[i] - factors[i - top] * wrow
                vs[i] = vs[i] - factors[i - top] * vrow
    out_l, out_v = [], []
    for i in range(2):
        scale = 1.0 / jnp.sqrt(diagonal[i])
        keep = (lanes() % 64 >= line + 8 * i) & (lanes() % 64 < 16)
        out_l.append(jnp.where(keep, ws[i] * scale, 0.0))
        out_v.append(vs[i] * scale)
    return out_l, jnp.concatenate(out_v, axis=0)


def pack_rows(top, bottom, s):
    out = []
    for part in (top, bottom):
        part = part if s == 0 else pltpu.roll(part, 64, 1)
        part = pltpu.roll(jnp.where(lanes() < 16, part, 0.0), 0, 1, stride=16, stride_axis=0)
        out.append(jnp.sum(part, axis=0, keepdims=True))
    return out


def make_table(me, receivers, transmitters, counts, interferers):
    lane = lax.broadcasted_iota(jnp.int32, (1, 256), 1)
    listed = interferers
    number = lax.broadcasted_iota(jnp.int32, (40, 256), 0)
    used = number < counts
    link, apart, slots, wanted, served = jnp.zeros((1, 256), jnp.int32), [], [], [], []
    for s in range(2):
        mine = lane == 2 * me + s
        cell = jnp.sum(jnp.where(mine, receivers, 0), axis=1, keepdims=True)
        column = jnp.max(jnp.where(mine & used, listed, -1), axis=1, keepdims=True)
        match = (column == transmitters).astype(jnp.int32)
        own = (cell == transmitters).astype(jnp.int32)
        apart.append(jnp.sum(match, axis=0, keepdims=True))
        link = link + jnp.sum(match * (number + (1 + 41 * s)), axis=0, keepdims=True) + own * (41 * s)
        slots.append(jnp.sum(own * lane, axis=1, keepdims=True))
        if s == 1:
            second = apart[1] + own
        cell = jnp.sum(jnp.where(mine, transmitters, 0), axis=1, keepdims=True)
        own = (cell == receivers).astype(jnp.int32)
        wanted.append(jnp.max((used & (listed == cell)).astype(jnp.int32), axis=0, keepdims=True) + own)
        served.append(jnp.sum(own * lane, axis=1, keepdims=True))
    misc = sum(jnp.where(lane == i, v, 0) for i, v in enumerate(slots + served))
    rows = [link, apart[0], apart[1], wanted[0], wanted[1], second]
    rows = [r + pltpu.roll(r, 255, 1) for r in rows] + [misc, misc]
    return [jnp.clip(r, 0, top) for r, top in zip(rows, (81, 1, 1, 1, 1, 1, 255, 255))]


def kernel(
    receivers, transmitters, counts, interferers, channels, first_precoders, precoders_out, weights_out,
    raw, links, current, psend, parr, gbuf, fsend, farr, lsend, larr, pair, acc1, acc2, tabv, tab,
    raw_sem, tab_sem, psend_sem, precv, fsend_sem, frecv, lsend_sem, lrecv,
):
    me = lax.axis_index("cells")
    mz, mx, my, mc = me // 32, (me // 8) % 4, (me // 2) % 4, me % 2

    zs = [lax.rem(mz + a, 4) * 32 for a in range(4)]
    xs = [lax.rem(mx + a, 4) * 8 for a in range(4)]
    ys = [lax.rem(my + a, 4) * 2 for a in range(4)]
    cs = [mc, 1 - mc]

    def target(k):
        dz, dx, dy, dc = OFFSETS[k]
        return zs[dz] + xs[dx] + ys[dy] + cs[dc]

    def source(k):
        dz, dx, dy, dc = OFFSETS[k]
        return zs[(4 - dz) % 4] + xs[(4 - dx) % 4] + ys[(4 - dy) % 4] + cs[dc]

    def slot_from(d):
        z, x, y, c = d // 32, (d // 8) % 4, (d // 2) % 4, d % 2
        return (((mz + 4 - z) % 4 * 4 + (mx + 4 - x) % 4) * 4 + (my + 4 - y) % 4) * 2 + (mc + 2 - c) % 2

    def copy(src, dst, i, send, recv):
        return pltpu.make_async_remote_copy(
            src_ref=src, dst_ref=dst, send_sem=send, recv_sem=recv,
            device_id=(target(i),), device_id_type=MESH,
        )

    remote = pl.ds(1, DEV - 1)

    def wait_group(buf, g, send, recv):
        part = buf.at[pl.ds(1, SIZES[g] - (g == LAST))]
        copy(part, part, ORDER[0], send, recv.at[g]).wait_recv()

    fetch = pltpu.make_async_copy(channels, raw, raw_sem)
    fetch.start()
    barrier = pltpu.get_barrier_semaphore()

    for k in ORDER[: DEV - 1]:
        pl.semaphore_signal(barrier, inc=1, device_id=(target(k),), device_id_type=MESH)
    current[...] = first_precoders[...]
    table = make_table(me, receivers[...], transmitters[...], counts[...], interferers[...])
    for i in range(8):
        tabv[i : i + 1, :] = table[i]
    lookup = pltpu.make_async_copy(tabv, tab, tab_sem)
    lookup.start()
    half = lax.broadcasted_iota(jnp.int32, (16, 128), 1) < 64
    left = lax.broadcasted_iota(jnp.int32, (64, 128), 1) < 64

    def prepare(i, carry):
        high, low = split(raw[i])
        links[i, 0:64, :] = high
        links[i, 64:128, :] = low
        return carry

    fetch.wait()
    lax.fori_loop(0, 82, prepare, 0)
    lookup.wait()
    pl.semaphore_wait(barrier, DEV - 1)

    def layer(index, carry):
        for g, members in enumerate(GROUPS):
            for k in members:
                psend[k] = current[tab[4, 2 * target(k)]]
            for k in members:
                if k > 0:
                    copy(psend.at[k], parr.at[k], k, psend_sem, precv.at[g]).start()
        parr[0] = psend[0]

        for g, members in enumerate(GROUPS):
            wait_group(parr, g, psend_sem, precv)
            highs, lows = [], []
            for i in members:
                d = source(i)
                high, low = split(parr[i])
                product = mm(jnp.concatenate([high, low], axis=0), links[tab[0, 2 * d]], NT)
                total = product[0:16] + product[16:32]
                total = total + pltpu.roll(total, 64, 1)
                gbuf[i] = total
                masked = total * jnp.where(half, tab[1, 2 * d].astype(F32), tab[2, 2 * d].astype(F32))
                high, low = split(masked)
                highs.append(high)
                lows.append(low)
            high, low = jnp.concatenate(highs, axis=0), jnp.concatenate(lows, axis=0)
            one, two = mm(high, high, TN), mm(high, low, TN)
            acc1[:, 0:128] = one if g == 0 else acc1[:, 0:128] + one
            acc2[:, 0:128] = two if g == 0 else acc2[:, 0:128] + two

        cross = acc2[:, 0:128]
        full = acc1[:, 0:128] + cross + cross.T
        line = lax.broadcasted_iota(jnp.int32, (64, 128), 0)
        spot = lax.broadcasted_iota(jnp.int32, (64, 128), 1) % 64
        covariance = jnp.where(left, full[0:64], full[64:128]) + (line == spot).astype(F32)
        direct = jnp.where(half, gbuf[slot_from(tab[6, 0] // 2)], gbuf[slot_from(tab[6, 1] // 2)])
        v = jnp.concatenate(right_divide(rows_of(covariance) + rows_of(direct))[0:2], axis=0)
        blank = jnp.zeros((48, 128), F32)
        apart = jnp.concatenate(
            [jnp.where(half, direct, 0.0), blank, jnp.where(half, 0.0, direct), blank], axis=0
        )
        short = lax.broadcasted_iota(jnp.int32, (16, 128), 0)
        w = mm_exact(v, apart, NT)
        w = w + (lax.broadcasted_iota(jnp.int32, (16, 128), 1) % 64 == short).astype(F32)
        for s in range(2):
            for i, row in enumerate(pack_rows(w[0:8], w[8:16], s)):
                weights_out[s : s + 1, 128 * i : 128 * i + 128] = row
        lower, filters = lower_divide(w, v)
        for s in range(2):
            mine = jnp.where(half, filters, 0.0) if s == 0 else jnp.where(half, 0.0, filters)
            mine = mine + pltpu.roll(mine, 64, 1)
            high, low = split(mine)
            pair[s] = jnp.concatenate([high, low], axis=0)
        for s in range(2):
            for i, row in enumerate(pack_rows(lower[0], lower[1], s)):
                lsend[2 * s + i : 2 * s + i + 1, :] = row
        larr[0] = lsend[...]

        for g, members in enumerate(GROUPS):
            for k in members:
                d = 2 * target(k)
                product = mm(pair[tab[5, d]], links[tab[0, d]], NN)
                fsend[k] = product[0:16] + product[16:32]
            for k in members:
                if k > 0:
                    copy(fsend.at[k], farr.at[k], k, fsend_sem, frecv.at[g]).start()
        farr[0] = fsend[0]

        for g, members in enumerate(GROUPS):
            if g == LATE:
                for k in ORDER[: DEV - 1]:
                    copy(lsend, larr.at[k], k, lsend_sem, lrecv).start()
            wait_group(farr, g, fsend_sem, frecv)
            highs, lows, highs01, lows01 = [], [], [], []
            for i in members:
                d = source(i)
                m0, m1 = tab[3, 2 * d].astype(F32), tab[4, 2 * d].astype(F32)
                f = farr[i]
                highs.append(f.astype(BF16))
                high, low = split(jnp.concatenate([f * m0, f * m1], axis=1))
                highs01.append(high)
                lows01.append(low)
            high = jnp.concatenate(highs, axis=0)
            one = mm(high, jnp.concatenate(highs01, axis=0), TN)
            two = mm(high, jnp.concatenate(lows01, axis=0), TN)
            acc1[...] = one if g == 0 else acc1[...] + one
            acc2[...] = two if g == 0 else acc2[...] + two

        mu = jnp.where(index == 0, STEP_SIZES[0], jnp.where(index == 1, STEP_SIZES[1], jnp.where(index == 2, STEP_SIZES[2], STEP_SIZES[3]))).astype(F32)
        eye = (
            lax.broadcasted_iota(jnp.int32, (128, 128), 0) == lax.broadcasted_iota(jnp.int32, (128, 128), 1)
        ).astype(F32) * mu
        systems = []
        for t in range(2):
            cross = acc2[:, 128 * t : 128 * t + 128]
            systems.append(acc1[:, 128 * t : 128 * t + 128] + cross + cross.T + eye)
        a0, a1 = systems
        steps = [slot_from(tab[6, 2 + t] // 2) for t in range(2)]
        b0, b1 = farr[steps[0]], farr[steps[1]]
        upper = jnp.where(left, a0[0:64], a1[64:128])
        under = jnp.where(left, a0[64:128], a1[0:64])
        inverse = invert(rows_of(upper))
        diagonal = jnp.concatenate([jnp.where(left, inverse, 0.0), jnp.where(left, 0.0, inverse)], axis=0)
        solved = mm_split(jnp.concatenate([under, jnp.where(half, b0, b1)], axis=0), diagonal, NN)
        beside = jnp.concatenate([jnp.where(left, 0.0, a0[0:64]), jnp.where(left, a1[64:128], 0.0)], axis=0)
        update = mm_split(solved, beside, NN)
        rest = jnp.where(left, a1[0:64], a0[64:128]) - update[0:64]
        side = jnp.where(half, b1, b0) - update[64:80]
        second = jnp.concatenate(right_divide(rows_of(rest) + rows_of(side))[0:2], axis=0)
        under = solved[0:64]
        back = jnp.concatenate([jnp.where(left, 0.0, under), jnp.where(left, under, 0.0)], axis=0)
        first = solved[64:80] - mm_split(second, back, NN)
        answers = [jnp.where(half, first, second), jnp.where(half, second, first)]

        lowers = copy(larr.at[remote], larr.at[remote], ORDER[0], lsend_sem, lrecv)
        lowers.wait_recv()
        lowers.wait_send()
        copy(psend.at[remote], parr.at[remote], ORDER[0], psend_sem, precv.at[0]).wait_send()
        copy(fsend.at[remote], farr.at[remote], ORDER[0], fsend_sem, frecv.at[0]).wait_send()
        low16 = lanes() < 16
        unpack = (lanes() + 16 * lax.broadcasted_iota(jnp.int32, (8, 128), 0)) % 128
        for t in range(2):
            got = larr[steps[t]]
            got = jnp.where(tab[6, 2 + t] % 2 == 0, got[0:2], got[2:4])
            triangle = jnp.concatenate(
                [
                    jnp.where(low16, jnp.take_along_axis(pick_row(got, i), unpack, axis=1), 0.0)
                    for i in range(2)
                ],
                axis=0,
            )
            current[t] = mm_exact(triangle, answers[t], TN)[0:16]
        return carry

    lax.fori_loop(0, LAYERS, layer, 0)
    precoders_out[...] = current[...]


def body(channels, precoders_init, receiver_cells, transmitter_cells, interferers, counts):
    dma = pltpu.SemaphoreType.DMA
    vmem = pl.BlockSpec(memory_space=pltpu.VMEM)
    slots = pltpu.VMEM((DEV, 16, 128), F32)
    return pl.pallas_call(
        kernel,
        out_shape=(
            jax.ShapeDtypeStruct((2, 16, 128), F32),
            jax.ShapeDtypeStruct((2, 256), F32),
        ),
        in_specs=[vmem, vmem, vmem, vmem, pl.BlockSpec(memory_space=pl.ANY), vmem],
        out_specs=(vmem, vmem),
        scratch_shapes=[
            pltpu.VMEM((82, 64, 128), F32),
            pltpu.VMEM((82, 128, 128), BF16),
            pltpu.VMEM((2, 16, 128), F32),
            slots, slots, slots, slots, slots,
            pltpu.VMEM((4, 128), F32),
            pltpu.VMEM((DEV, 4, 128), F32),
            pltpu.VMEM((2, 32, 128), BF16),
            pltpu.VMEM((128, 256), F32),
            pltpu.VMEM((128, 256), F32),
            pltpu.VMEM((8, 256), jnp.int32),
            pltpu.SMEM((8, 256), jnp.int32),
            dma, dma, dma, dma((len(GROUPS),)), dma, dma((len(GROUPS),)), dma, dma,
        ],
        compiler_params=pltpu.CompilerParams(collective_id=0, has_side_effects=True),
    )(
        receiver_cells.reshape(1, 256), transmitter_cells.reshape(1, 256), counts.reshape(1, 256), interferers.T,
        channels.reshape(82, 64, 128), precoders_init,
    )


def solution(mesh):
    return jax.shard_map(
        body,
        mesh=mesh,
        in_specs=(P("cells", None, None, None), P("cells", None, None), P(), P(), P(), P()),
        out_specs=(P("cells", None, None), P("cells", None)),
        check_vma=False,
    )
```

```python
import random

import jax
import jax.numpy as jnp
from jax import lax
from jax.experimental import pallas as pl
from jax.experimental.pallas import tpu as pltpu
from jax.sharding import PartitionSpec as P

LAYERS = 4
STEP_SIZES = (0.3, 0.2, 0.15, 0.1)
HIGHEST = lax.Precision.HIGHEST
MESH = pl.DeviceIdType.MESH
F32, BF16 = jnp.float32, jnp.bfloat16
DEV = 128
OFFSETS = [(z, x, y, c) for z in range(4) for x in range(4) for y in range(4) for c in range(2)]
shuffled = random.Random(5)
ORDER = sorted(range(DEV), key=lambda i: (-sum(min(a, 4 - a) for a in OFFSETS[i][:3]), -i if i < 2 else shuffled.random()))
SIZES = [8, 8, 16, 16, 16, 16, 16, 16, 8, 8]
GROUPS = [ORDER[sum(SIZES[:g]) : sum(SIZES[: g + 1])] for g in range(len(SIZES))]
LAST = len(GROUPS) - 1
NN = (((1,), (0,)), ((), ()))
NT = (((1,), (1,)), ((), ()))
TN = (((0,), (0,)), ((), ()))


def split(x):
    high = x.astype(BF16)
    return high, (x - high.astype(F32)).astype(BF16)


def mm(a, b, dims):
    return lax.dot_general(a, b, dims, preferred_element_type=F32)


def mm_exact(a, b, dims):
    return lax.dot_general(a, b, dims, precision=HIGHEST, preferred_element_type=F32)


def mm_split(a, b, dims):
    (ah, al), (bh, bl) = split(a), split(b)
    return mm(ah, bh, dims) + (mm(ah, bl, dims) + mm(al, bh, dims))


def lanes():
    return lax.broadcasted_iota(jnp.int32, (8, 128), 1)


def pick_row(v, row):
    return jnp.broadcast_to(v[row : row + 1, :], (8, 128))


def pick_lane(v, k):
    return jnp.take_along_axis(v, jnp.where(lanes() < 64, k, 64 + k), axis=1)


def rows_of(x):
    return [x[8 * i : 8 * i + 8, :] for i in range(x.shape[0] // 8)]


def clear_block(rows, top, others):
    spot, line = lanes() % 64, lax.broadcasted_iota(jnp.int32, (8, 128), 0)
    columns = [pick_lane(rows[top], 8 * top + j) for j in range(8)]
    unit = (spot == line + 8 * top).astype(F32)
    x = rows[top] - unit
    for j in range(0, 8, 2):
        a, b = columns[j], columns[j + 1]
        p11, p21, p12, p22 = pick_row(a, j), pick_row(a, j + 1), pick_row(b, j), pick_row(b, j + 1)
        inverse = 1.0 / (p11 * p22 - p12 * p21)
        a, b = a - (line == j).astype(F32), b - (line == j + 1).astype(F32)
        one, two = (a * p22 - b * p21) * inverse, (b * p11 - a * p12) * inverse
        for later in range(j + 2, 8):
            column = columns[later]
            columns[later] = column - one * pick_row(column, j) - two * pick_row(column, j + 1)
        x = x - one * pick_row(x, j) - two * pick_row(x, j + 1)
    pivots = [pick_row(x, j) for j in range(8)]
    for i in others:
        t = [pick_lane(rows[i], 8 * top + j) * pivots[j] for j in range(8)]
        rows[i] = rows[i] - (((t[0] + t[1]) + (t[2] + t[3])) + ((t[4] + t[5]) + (t[6] + t[7])))
    rows[top] = unit - x


def right_divide(rows):
    rows = list(rows)
    for top in range(8):
        clear_block(rows, top, range(top + 1, len(rows)))
    return rows[8:]


def invert(rows):
    rows = list(rows)
    for top in range(8):
        clear_block(rows, top, [i for i in range(8) if i != top])
    return jnp.concatenate(rows, axis=0)


def lower_divide(w, v):
    ws, vs = rows_of(w), rows_of(v)
    line = lax.broadcasted_iota(jnp.int32, (8, 128), 0)
    diagonal = [jnp.ones((8, 128), F32), jnp.ones((8, 128), F32)]
    for top in range(2):
        columns = [[pick_lane(ws[i], 8 * top + j) for i in range(top, 2)] for j in range(8)]
        for j in range(8):
            pivot = pick_row(columns[j][0], j)
            inverse = 1.0 / pivot
            factors = [c * inverse for c in columns[j]]
            factors[0] = jnp.where(line > j, factors[0], 0.0)
            diagonal[top] = jnp.where(line == j, pivot, diagonal[top])
            for later in range(j + 1, 8):
                row = pick_row(columns[later][0], j)
                columns[later] = [c - f * row for c, f in zip(columns[later], factors)]
            wrow, vrow = pick_row(ws[top], j), pick_row(vs[top], j)
            for i in range(top, 2):
                ws[i] = ws[i] - factors[i - top] * wrow
                vs[i] = vs[i] - factors[i - top] * vrow
    out_l, out_v = [], []
    for i in range(2):
        scale = 1.0 / jnp.sqrt(diagonal[i])
        keep = (lanes() % 64 >= line + 8 * i) & (lanes() % 64 < 16)
        out_l.append(jnp.where(keep, ws[i] * scale, 0.0))
        out_v.append(vs[i] * scale)
    return out_l, jnp.concatenate(out_v, axis=0)


def pack_rows(top, bottom, s):
    out = []
    for part in (top, bottom):
        part = part if s == 0 else pltpu.roll(part, 64, 1)
        part = pltpu.roll(jnp.where(lanes() < 16, part, 0.0), 0, 1, stride=16, stride_axis=0)
        out.append(jnp.sum(part, axis=0, keepdims=True))
    return out


def make_table(me, receivers, transmitters, counts, interferers):
    lane = lax.broadcasted_iota(jnp.int32, (1, 256), 1)
    listed = interferers
    number = lax.broadcasted_iota(jnp.int32, (40, 256), 0)
    used = number < counts
    link, apart, slots, wanted, served = jnp.zeros((1, 256), jnp.int32), [], [], [], []
    for s in range(2):
        mine = lane == 2 * me + s
        cell = jnp.sum(jnp.where(mine, receivers, 0), axis=1, keepdims=True)
        column = jnp.max(jnp.where(mine & used, listed, -1), axis=1, keepdims=True)
        match = (column == transmitters).astype(jnp.int32)
        own = (cell == transmitters).astype(jnp.int32)
        apart.append(jnp.sum(match, axis=0, keepdims=True))
        link = link + jnp.sum(match * (number + (1 + 41 * s)), axis=0, keepdims=True) + own * (41 * s)
        slots.append(jnp.sum(own * lane, axis=1, keepdims=True))
        if s == 1:
            second = apart[1] + own
        cell = jnp.sum(jnp.where(mine, transmitters, 0), axis=1, keepdims=True)
        own = (cell == receivers).astype(jnp.int32)
        wanted.append(jnp.max((used & (listed == cell)).astype(jnp.int32), axis=0, keepdims=True) + own)
        served.append(jnp.sum(own * lane, axis=1, keepdims=True))
    misc = sum(jnp.where(lane == i, v, 0) for i, v in enumerate(slots + served))
    rows = [link, apart[0], apart[1], wanted[0], wanted[1], second]
    rows = [r + pltpu.roll(r, 255, 1) for r in rows] + [misc, misc]
    return [jnp.clip(r, 0, top) for r, top in zip(rows, (81, 1, 1, 1, 1, 1, 255, 255))]


def kernel(
    receivers, transmitters, counts, interferers, channels, first_precoders, precoders_out, weights_out,
    raw, links, current, psend, parr, gbuf, fsend, farr, lower_rows, pair, acc1, tabv, tab,
    raw_sem, tab_sem, psend_sem, precv, fsend_sem, frecv,
):
    me = lax.axis_index("cells")
    mz, mx, my, mc = me // 32, (me // 8) % 4, (me // 2) % 4, me % 2

    zs = [lax.rem(mz + a, 4) * 32 for a in range(4)]
    xs = [lax.rem(mx + a, 4) * 8 for a in range(4)]
    ys = [lax.rem(my + a, 4) * 2 for a in range(4)]
    cs = [mc, 1 - mc]

    def target(k):
        dz, dx, dy, dc = OFFSETS[k]
        return zs[dz] + xs[dx] + ys[dy] + cs[dc]

    def source(k):
        dz, dx, dy, dc = OFFSETS[k]
        return zs[(4 - dz) % 4] + xs[(4 - dx) % 4] + ys[(4 - dy) % 4] + cs[dc]

    def slot_from(d):
        z, x, y, c = d // 32, (d // 8) % 4, (d // 2) % 4, d % 2
        return (((mz + 4 - z) % 4 * 4 + (mx + 4 - x) % 4) * 4 + (my + 4 - y) % 4) * 2 + (mc + 2 - c) % 2

    def copy(src, dst, i, send, recv):
        return pltpu.make_async_remote_copy(
            src_ref=src, dst_ref=dst, send_sem=send, recv_sem=recv,
            device_id=(target(i),), device_id_type=MESH,
        )

    remote = pl.ds(1, DEV - 1)

    def wait_group(buf, g, send, recv):
        part = buf.at[pl.ds(1, SIZES[g] - (g == LAST))]
        copy(part, part, ORDER[0], send, recv.at[g]).wait_recv()

    fetch = pltpu.make_async_copy(channels, raw, raw_sem)
    fetch.start()
    barrier = pltpu.get_barrier_semaphore()

    for k in ORDER[: DEV - 1]:
        pl.semaphore_signal(barrier, inc=1, device_id=(target(k),), device_id_type=MESH)
    current[...] = first_precoders[...]
    table = make_table(me, receivers[...], transmitters[...], counts[...], interferers[...])
    for i in range(8):
        tabv[i : i + 1, :] = table[i]
    lookup = pltpu.make_async_copy(tabv, tab, tab_sem)
    lookup.start()
    half = lax.broadcasted_iota(jnp.int32, (16, 128), 1) < 64
    left = lax.broadcasted_iota(jnp.int32, (64, 128), 1) < 64

    def prepare(i, carry):
        high, low = split(raw[i])
        links[i, 0:64, :] = high
        links[i, 64:128, :] = low
        return carry

    fetch.wait()
    lax.fori_loop(0, 82, prepare, 0)
    lookup.wait()
    pl.semaphore_wait(barrier, DEV - 1)

    def layer(index, carry):
        for g, members in enumerate(GROUPS):
            for k in members:
                psend[k] = current[tab[4, 2 * target(k)]]
            for k in members:
                if k > 0:
                    copy(psend.at[k], parr.at[k], k, psend_sem, precv.at[g]).start()
        parr[0] = psend[0]

        for g, members in enumerate(GROUPS):
            wait_group(parr, g, psend_sem, precv)
            highs, lows = [], []
            for i in members:
                d = source(i)
                high, low = split(parr[i])
                product = mm(jnp.concatenate([high, low], axis=0), links[tab[0, 2 * d]], NT)
                total = product[0:16] + product[16:32]
                total = total + pltpu.roll(total, 64, 1)
                gbuf[i] = total
                masked = total * jnp.where(half, tab[1, 2 * d].astype(F32), tab[2, 2 * d].astype(F32))
                high, low = split(masked)
                highs.append(high)
                lows.append(low)
            high, low = jnp.concatenate(highs, axis=0), jnp.concatenate(lows, axis=0)
            one = mm(high, high, TN) + (mm(high, low, TN) + mm(low, high, TN))
            acc1[:, 0:128] = one if g == 0 else acc1[:, 0:128] + one

        full = acc1[:, 0:128]
        line = lax.broadcasted_iota(jnp.int32, (64, 128), 0)
        spot = lax.broadcasted_iota(jnp.int32, (64, 128), 1) % 64
        covariance = jnp.where(left, full[0:64], full[64:128]) + (line == spot).astype(F32)
        direct = jnp.where(half, gbuf[slot_from(tab[6, 0] // 2)], gbuf[slot_from(tab[6, 1] // 2)])
        v = jnp.concatenate(right_divide(rows_of(covariance) + rows_of(direct))[0:2], axis=0)
        blank = jnp.zeros((48, 128), F32)
        apart = jnp.concatenate(
            [jnp.where(half, direct, 0.0), blank, jnp.where(half, 0.0, direct), blank], axis=0
        )
        short = lax.broadcasted_iota(jnp.int32, (16, 128), 0)
        w = mm_split(v, apart, NT)
        w = w + (lax.broadcasted_iota(jnp.int32, (16, 128), 1) % 64 == short).astype(F32)
        for s in range(2):
            for i, row in enumerate(pack_rows(w[0:8], w[8:16], s)):
                weights_out[s : s + 1, 128 * i : 128 * i + 128] = row
        lower, filters = lower_divide(w, v)
        for s in range(2):
            mine = jnp.where(half, filters, 0.0) if s == 0 else jnp.where(half, 0.0, filters)
            mine = mine + pltpu.roll(mine, 64, 1)
            high, low = split(mine)
            pair[s] = jnp.concatenate([high, low], axis=0)
        for s in range(2):
            for i, row in enumerate(pack_rows(lower[0], lower[1], s)):
                lower_rows[s, i : i + 1, :] = row

        for g, members in enumerate(GROUPS):
            for k in members:
                d = 2 * target(k)
                product = mm(pair[tab[5, d]], links[tab[0, d]], NN)
                fsend[k, 0:16, :] = product[0:16] + product[16:32]
                fsend[k, 16:18, :] = lower_rows[tab[5, d]]
            for k in members:
                if k > 0:
                    copy(fsend.at[k], farr.at[k], k, fsend_sem, frecv.at[g]).start()
        farr[0] = fsend[0]

        for g, members in enumerate(GROUPS):
            wait_group(farr, g, fsend_sem, frecv)
            highs, lows, highs01, lows01 = [], [], [], []
            for i in members:
                d = source(i)
                m0, m1 = tab[3, 2 * d].astype(F32), tab[4, 2 * d].astype(F32)
                f = farr[i, 0:16, :]
                high, low = split(f)
                highs.append(high)
                lows.append(low)
                high, low = split(jnp.concatenate([f * m0, f * m1], axis=1))
                highs01.append(high)
                lows01.append(low)
            high, low = jnp.concatenate(highs, axis=0), jnp.concatenate(lows, axis=0)
            high01, low01 = jnp.concatenate(highs01, axis=0), jnp.concatenate(lows01, axis=0)
            one = mm(high, high01, TN) + (mm(high, low01, TN) + mm(low, high01, TN))
            acc1[...] = one if g == 0 else acc1[...] + one

        mu = jnp.where(index == 0, STEP_SIZES[0], jnp.where(index == 1, STEP_SIZES[1], jnp.where(index == 2, STEP_SIZES[2], STEP_SIZES[3]))).astype(F32)
        eye = (
            lax.broadcasted_iota(jnp.int32, (128, 128), 0) == lax.broadcasted_iota(jnp.int32, (128, 128), 1)
        ).astype(F32) * mu
        a0, a1 = acc1[:, 0:128] + eye, acc1[:, 128:256] + eye
        steps = [slot_from(tab[6, 2 + t] // 2) for t in range(2)]
        low16 = lanes() < 16
        unpack = (lanes() + 16 * lax.broadcasted_iota(jnp.int32, (8, 128), 0)) % 128
        sides = []
        for t in range(2):
            got = farr[steps[t], 16:18, :]
            triangle = jnp.concatenate(
                [
                    jnp.where(low16, jnp.take_along_axis(pick_row(got, i), unpack, axis=1), 0.0)
                    for i in range(2)
                ],
                axis=0,
            )
            sides.append(mm_exact(triangle, farr[steps[t], 0:16, :], TN)[0:16])
        b0, b1 = sides
        upper = jnp.where(left, a0[0:64], a1[64:128])
        under = jnp.where(left, a0[64:128], a1[0:64])
        inverse = invert(rows_of(upper))
        diagonal = jnp.concatenate([jnp.where(left, inverse, 0.0), jnp.where(left, 0.0, inverse)], axis=0)
        solved = mm_split(jnp.concatenate([under, jnp.where(half, b0, b1)], axis=0), diagonal, NN)
        beside = jnp.concatenate([jnp.where(left, 0.0, a0[0:64]), jnp.where(left, a1[64:128], 0.0)], axis=0)
        update = mm_split(solved, beside, NN)
        rest = jnp.where(left, a1[0:64], a0[64:128]) - update[0:64]
        side = jnp.where(half, b1, b0) - update[64:80]
        second = jnp.concatenate(right_divide(rows_of(rest) + rows_of(side))[0:2], axis=0)
        under = solved[0:64]
        back = jnp.concatenate([jnp.where(left, 0.0, under), jnp.where(left, under, 0.0)], axis=0)
        first = solved[64:80] - mm_split(second, back, NN)
        copy(psend.at[remote], parr.at[remote], ORDER[0], psend_sem, precv.at[0]).wait_send()
        copy(fsend.at[remote], farr.at[remote], ORDER[0], fsend_sem, frecv.at[0]).wait_send()
        current[0] = jnp.where(half, first, second)
        current[1] = jnp.where(half, second, first)
        return carry

    lax.fori_loop(0, LAYERS, layer, 0)
    precoders_out[...] = current[...]


def copy_kernel(a_in, b_in, a_out, b_out):
    a_out[...] = a_in[...]
    b_out[...] = b_in[...]


def body(channels, precoders_init, receiver_cells, transmitter_cells, interferers, counts):
    dma = pltpu.SemaphoreType.DMA
    vmem = pl.BlockSpec(memory_space=pltpu.VMEM)
    slots, wide = pltpu.VMEM((DEV, 16, 128), F32), pltpu.VMEM((DEV, 18, 128), F32)
    shapes = (jax.ShapeDtypeStruct((2, 16, 128), F32), jax.ShapeDtypeStruct((2, 256), F32))
    results = pl.pallas_call(
        kernel,
        out_shape=shapes,
        in_specs=[vmem, vmem, vmem, vmem, pl.BlockSpec(memory_space=pl.ANY), vmem],
        out_specs=(vmem, vmem),
        scratch_shapes=[
            pltpu.VMEM((82, 64, 128), F32),
            pltpu.VMEM((82, 128, 128), BF16),
            pltpu.VMEM((2, 16, 128), F32),
            slots, slots, slots, wide, wide,
            pltpu.VMEM((2, 2, 128), F32),
            pltpu.VMEM((2, 32, 128), BF16),
            pltpu.VMEM((128, 256), F32),
            pltpu.VMEM((8, 256), jnp.int32),
            pltpu.SMEM((8, 256), jnp.int32),
            dma, dma, dma, dma((len(GROUPS),)), dma, dma((len(GROUPS),)),
        ],
        compiler_params=pltpu.CompilerParams(collective_id=0, has_side_effects=True),
    )(
        receiver_cells.reshape(1, 256), transmitter_cells.reshape(1, 256), counts.reshape(1, 256), interferers.T,
        channels.reshape(82, 64, 128), precoders_init,
    )
    return pl.pallas_call(copy_kernel, out_shape=shapes, in_specs=[vmem, vmem], out_specs=(vmem, vmem))(*results)


def solution(mesh):
    return jax.shard_map(
        body,
        mesh=mesh,
        in_specs=(P("cells", None, None, None), P("cells", None, None), P(), P(), P(), P()),
        out_specs=(P("cells", None, None), P("cells", None)),
        check_vma=False,
    )
```

```python
import random

import jax
import jax.numpy as jnp
from jax import lax
from jax.experimental import pallas as pl
from jax.experimental.pallas import tpu as pltpu
from jax.sharding import PartitionSpec as P

LAYERS = 4
STEP_SIZES = (0.3, 0.2, 0.15, 0.1)
HIGHEST = lax.Precision.HIGHEST
MESH = pl.DeviceIdType.MESH
F32, BF16 = jnp.float32, jnp.bfloat16
DEV = 128
OFFSETS = [(z, x, y, c) for z in range(4) for x in range(4) for y in range(4) for c in range(2)]
shuffled = random.Random(5)
ORDER = sorted(range(DEV), key=lambda i: (-sum(min(a, 4 - a) for a in OFFSETS[i][:3]), -i if i < 2 else shuffled.random()))
SIZES = [16, 16, 16, 16, 32, 32]
GROUPS = [ORDER[sum(SIZES[:g]) : sum(SIZES[: g + 1])] for g in range(len(SIZES))]
LAST = len(GROUPS) - 1
NN = (((1,), (0,)), ((), ()))
NT = (((1,), (1,)), ((), ()))
TN = (((0,), (0,)), ((), ()))


def split(x):
    high = x.astype(BF16)
    return high, (x - high.astype(F32)).astype(BF16)


def mm(a, b, dims):
    return lax.dot_general(a, b, dims, preferred_element_type=F32)


def mm_exact(a, b, dims):
    return lax.dot_general(a, b, dims, precision=HIGHEST, preferred_element_type=F32)


def mm_split(a, b, dims):
    (ah, al), (bh, bl) = split(a), split(b)
    return mm(ah, bh, dims) + (mm(ah, bl, dims) + mm(al, bh, dims))


def lanes():
    return lax.broadcasted_iota(jnp.int32, (8, 128), 1)


def pick_row(v, row):
    return jnp.broadcast_to(v[row : row + 1, :], (8, 128))


def pick_lane(v, k):
    return jnp.take_along_axis(v, jnp.where(lanes() < 64, k, 64 + k), axis=1)


def rows_of(x):
    return [x[8 * i : 8 * i + 8, :] for i in range(x.shape[0] // 8)]


def clear_block(rows, top, others):
    spot, line = lanes() % 64, lax.broadcasted_iota(jnp.int32, (8, 128), 0)
    columns = [pick_lane(rows[top], 8 * top + j) for j in range(8)]
    unit = (spot == line + 8 * top).astype(F32)
    x = rows[top] - unit
    for j in range(0, 8, 2):
        a, b = columns[j], columns[j + 1]
        p11, p21, p12, p22 = pick_row(a, j), pick_row(a, j + 1), pick_row(b, j), pick_row(b, j + 1)
        inverse = 1.0 / (p11 * p22 - p12 * p21)
        a, b = a - (line == j).astype(F32), b - (line == j + 1).astype(F32)
        one, two = (a * p22 - b * p21) * inverse, (b * p11 - a * p12) * inverse
        for later in range(j + 2, 8):
            column = columns[later]
            columns[later] = column - one * pick_row(column, j) - two * pick_row(column, j + 1)
        x = x - one * pick_row(x, j) - two * pick_row(x, j + 1)
    pivots = [pick_row(x, j) for j in range(8)]
    for i in others:
        t = [pick_lane(rows[i], 8 * top + j) * pivots[j] for j in range(8)]
        rows[i] = rows[i] - (((t[0] + t[1]) + (t[2] + t[3])) + ((t[4] + t[5]) + (t[6] + t[7])))
    rows[top] = unit - x


def right_divide(rows):
    rows = list(rows)
    for top in range(8):
        clear_block(rows, top, range(top + 1, len(rows)))
    return rows[8:]


def invert(rows):
    rows = list(rows)
    for top in range(8):
        clear_block(rows, top, [i for i in range(8) if i != top])
    return jnp.concatenate(rows, axis=0)


def lower_divide(w, v):
    ws, vs = rows_of(w), rows_of(v)
    line = lax.broadcasted_iota(jnp.int32, (8, 128), 0)
    diagonal = [jnp.ones((8, 128), F32), jnp.ones((8, 128), F32)]
    for top in range(2):
        columns = [[pick_lane(ws[i], 8 * top + j) for i in range(top, 2)] for j in range(8)]
        for j in range(8):
            pivot = pick_row(columns[j][0], j)
            inverse = 1.0 / pivot
            factors = [c * inverse for c in columns[j]]
            factors[0] = jnp.where(line > j, factors[0], 0.0)
            diagonal[top] = jnp.where(line == j, pivot, diagonal[top])
            for later in range(j + 1, 8):
                row = pick_row(columns[later][0], j)
                columns[later] = [c - f * row for c, f in zip(columns[later], factors)]
            wrow, vrow = pick_row(ws[top], j), pick_row(vs[top], j)
            for i in range(top, 2):
                ws[i] = ws[i] - factors[i - top] * wrow
                vs[i] = vs[i] - factors[i - top] * vrow
    out_l, out_v = [], []
    for i in range(2):
        scale = 1.0 / jnp.sqrt(diagonal[i])
        keep = (lanes() % 64 >= line + 8 * i) & (lanes() % 64 < 16)
        out_l.append(jnp.where(keep, ws[i] * scale, 0.0))
        out_v.append(vs[i] * scale)
    return out_l, jnp.concatenate(out_v, axis=0)


def pack_rows(top, bottom, s):
    out = []
    for part in (top, bottom):
        part = part if s == 0 else pltpu.roll(part, 64, 1)
        part = pltpu.roll(jnp.where(lanes() < 16, part, 0.0), 0, 1, stride=16, stride_axis=0)
        out.append(jnp.sum(part, axis=0, keepdims=True))
    return out


def make_table(me, receivers, transmitters, counts, interferers):
    lane = lax.broadcasted_iota(jnp.int32, (1, 256), 1)
    listed = interferers
    number = lax.broadcasted_iota(jnp.int32, (40, 256), 0)
    used = number < counts
    link, apart, slots, wanted, served = jnp.zeros((1, 256), jnp.int32), [], [], [], []
    for s in range(2):
        mine = lane == 2 * me + s
        cell = jnp.sum(jnp.where(mine, receivers, 0), axis=1, keepdims=True)
        column = jnp.max(jnp.where(mine & used, listed, -1), axis=1, keepdims=True)
        match = (column == transmitters).astype(jnp.int32)
        own = (cell == transmitters).astype(jnp.int32)
        apart.append(jnp.sum(match, axis=0, keepdims=True))
        link = link + jnp.sum(match * (number + (1 + 41 * s)), axis=0, keepdims=True) + own * (41 * s)
        slots.append(jnp.sum(own * lane, axis=1, keepdims=True))
        if s == 1:
            second = apart[1] + own
        cell = jnp.sum(jnp.where(mine, transmitters, 0), axis=1, keepdims=True)
        own = (cell == receivers).astype(jnp.int32)
        wanted.append(jnp.max((used & (listed == cell)).astype(jnp.int32), axis=0, keepdims=True) + own)
        served.append(jnp.sum(own * lane, axis=1, keepdims=True))
    misc = sum(jnp.where(lane == i, v, 0) for i, v in enumerate(slots + served))
    rows = [link, apart[0], apart[1], wanted[0], wanted[1], second]
    rows = [r + pltpu.roll(r, 255, 1) for r in rows] + [misc, misc]
    return [jnp.clip(r, 0, top) for r, top in zip(rows, (81, 1, 1, 1, 1, 1, 255, 255))]


def kernel(
    receivers, transmitters, counts, interferers, channels, first_precoders, precoders_out, weights_out,
    raw, links, current, psend, parr, gbuf, fsend, farr, lower_rows, pair, acc1, tabv, tab,
    raw_sem, tab_sem, psend_sem, precv, fsend_sem, frecv,
):
    me = lax.axis_index("cells")
    mz, mx, my, mc = me // 32, (me // 8) % 4, (me // 2) % 4, me % 2

    zs = [lax.rem(mz + a, 4) * 32 for a in range(4)]
    xs = [lax.rem(mx + a, 4) * 8 for a in range(4)]
    ys = [lax.rem(my + a, 4) * 2 for a in range(4)]
    cs = [mc, 1 - mc]

    def target(k):
        dz, dx, dy, dc = OFFSETS[k]
        return zs[dz] + xs[dx] + ys[dy] + cs[dc]

    def source(k):
        dz, dx, dy, dc = OFFSETS[k]
        return zs[(4 - dz) % 4] + xs[(4 - dx) % 4] + ys[(4 - dy) % 4] + cs[dc]

    def slot_from(d):
        z, x, y, c = d // 32, (d // 8) % 4, (d // 2) % 4, d % 2
        return (((mz + 4 - z) % 4 * 4 + (mx + 4 - x) % 4) * 4 + (my + 4 - y) % 4) * 2 + (mc + 2 - c) % 2

    def copy(src, dst, i, send, recv):
        return pltpu.make_async_remote_copy(
            src_ref=src, dst_ref=dst, send_sem=send, recv_sem=recv,
            device_id=(target(i),), device_id_type=MESH,
        )

    remote = pl.ds(1, DEV - 1)

    def wait_group(buf, g, send, recv):
        part = buf.at[pl.ds(1, SIZES[g] - (g == LAST))]
        copy(part, part, ORDER[0], send, recv.at[g]).wait_recv()

    fetch = pltpu.make_async_copy(channels, raw, raw_sem)
    fetch.start()
    barrier = pltpu.get_barrier_semaphore()

    for k in ORDER[: DEV - 1]:
        pl.semaphore_signal(barrier, inc=1, device_id=(target(k),), device_id_type=MESH)
    current[...] = first_precoders[...]
    table = make_table(me, receivers[...], transmitters[...], counts[...], interferers[...])
    for i in range(8):
        tabv[i : i + 1, :] = table[i]
    lookup = pltpu.make_async_copy(tabv, tab, tab_sem)
    lookup.start()
    half = lax.broadcasted_iota(jnp.int32, (16, 128), 1) < 64
    left = lax.broadcasted_iota(jnp.int32, (64, 128), 1) < 64

    def prepare(i, carry):
        high, low = split(raw[i])
        links[i, 0:64, :] = high
        links[i, 64:128, :] = low
        return carry

    fetch.wait()
    lax.fori_loop(0, 82, prepare, 0)
    lookup.wait()
    pl.semaphore_wait(barrier, DEV - 1)

    def layer(index, carry):
        for g, members in enumerate(GROUPS):
            for k in members:
                psend[k] = current[tab[4, 2 * target(k)]]
            for k in members:
                if k > 0:
                    copy(psend.at[k], parr.at[k], k, psend_sem, precv.at[g]).start()
        parr[0] = psend[0]

        for g, members in enumerate(GROUPS):
            wait_group(parr, g, psend_sem, precv)
            highs, lows = [], []
            for i in members:
                d = source(i)
                high, low = split(parr[i])
                product = mm(jnp.concatenate([high, low], axis=0), links[tab[0, 2 * d]], NT)
                total = product[0:16] + product[16:32]
                total = total + pltpu.roll(total, 64, 1)
                gbuf[i] = total
                masked = total * jnp.where(half, tab[1, 2 * d].astype(F32), tab[2, 2 * d].astype(F32))
                high, low = split(masked)
                highs.append(high)
                lows.append(low)
            high, low = jnp.concatenate(highs, axis=0), jnp.concatenate(lows, axis=0)
            one = mm(high, high, TN) + (mm(high, low, TN) + mm(low, high, TN))
            acc1[:, 0:128] = one if g == 0 else acc1[:, 0:128] + one

        full = acc1[:, 0:128]
        line = lax.broadcasted_iota(jnp.int32, (64, 128), 0)
        spot = lax.broadcasted_iota(jnp.int32, (64, 128), 1) % 64
        covariance = jnp.where(left, full[0:64], full[64:128]) + (line == spot).astype(F32)
        direct = jnp.where(half, gbuf[slot_from(tab[6, 0] // 2)], gbuf[slot_from(tab[6, 1] // 2)])
        v = jnp.concatenate(right_divide(rows_of(covariance) + rows_of(direct))[0:2], axis=0)
        blank = jnp.zeros((48, 128), F32)
        apart = jnp.concatenate(
            [jnp.where(half, direct, 0.0), blank, jnp.where(half, 0.0, direct), blank], axis=0
        )
        short = lax.broadcasted_iota(jnp.int32, (16, 128), 0)
        w = mm_split(v, apart, NT)
        w = w + (lax.broadcasted_iota(jnp.int32, (16, 128), 1) % 64 == short).astype(F32)
        for s in range(2):
            for i, row in enumerate(pack_rows(w[0:8], w[8:16], s)):
                weights_out[s : s + 1, 128 * i : 128 * i + 128] = row
        lower, filters = lower_divide(w, v)
        for s in range(2):
            mine = jnp.where(half, filters, 0.0) if s == 0 else jnp.where(half, 0.0, filters)
            mine = mine + pltpu.roll(mine, 64, 1)
            high, low = split(mine)
            pair[s] = jnp.concatenate([high, low], axis=0)
        for s in range(2):
            for i, row in enumerate(pack_rows(lower[0], lower[1], s)):
                lower_rows[s, i : i + 1, :] = row

        for g, members in enumerate(GROUPS):
            for k in members:
                d = 2 * target(k)
                product = mm(pair[tab[5, d]], links[tab[0, d]], NN)
                fsend[k, 0:16, :] = product[0:16] + product[16:32]
                fsend[k, 16:18, :] = lower_rows[tab[5, d]]
            for k in members:
                if k > 0:
                    copy(fsend.at[k], farr.at[k], k, fsend_sem, frecv.at[g]).start()
        farr[0] = fsend[0]

        for g, members in enumerate(GROUPS):
            wait_group(farr, g, fsend_sem, frecv)
            highs, lows, highs01, lows01 = [], [], [], []
            for i in members:
                d = source(i)
                m0, m1 = tab[3, 2 * d].astype(F32), tab[4, 2 * d].astype(F32)
                f = farr[i, 0:16, :]
                high, low = split(f)
                highs.append(high)
                lows.append(low)
                high, low = split(jnp.concatenate([f * m0, f * m1], axis=1))
                highs01.append(high)
                lows01.append(low)
            high, low = jnp.concatenate(highs, axis=0), jnp.concatenate(lows, axis=0)
            high01, low01 = jnp.concatenate(highs01, axis=0), jnp.concatenate(lows01, axis=0)
            one = mm(high, high01, TN) + (mm(high, low01, TN) + mm(low, high01, TN))
            acc1[...] = one if g == 0 else acc1[...] + one

        mu = jnp.where(index == 0, STEP_SIZES[0], jnp.where(index == 1, STEP_SIZES[1], jnp.where(index == 2, STEP_SIZES[2], STEP_SIZES[3]))).astype(F32)
        eye = (
            lax.broadcasted_iota(jnp.int32, (128, 128), 0) == lax.broadcasted_iota(jnp.int32, (128, 128), 1)
        ).astype(F32) * mu
        a0, a1 = acc1[:, 0:128] + eye, acc1[:, 128:256] + eye
        steps = [slot_from(tab[6, 2 + t] // 2) for t in range(2)]
        low16 = lanes() < 16
        unpack = (lanes() + 16 * lax.broadcasted_iota(jnp.int32, (8, 128), 0)) % 128
        sides = []
        for t in range(2):
            got = farr[steps[t], 16:18, :]
            triangle = jnp.concatenate(
                [
                    jnp.where(low16, jnp.take_along_axis(pick_row(got, i), unpack, axis=1), 0.0)
                    for i in range(2)
                ],
                axis=0,
            )
            sides.append(mm_exact(triangle, farr[steps[t], 0:16, :], TN)[0:16])
        b0, b1 = sides
        upper = jnp.where(left, a0[0:64], a1[64:128])
        under = jnp.where(left, a0[64:128], a1[0:64])
        inverse = invert(rows_of(upper))
        diagonal = jnp.concatenate([jnp.where(left, inverse, 0.0), jnp.where(left, 0.0, inverse)], axis=0)
        solved = mm_split(jnp.concatenate([under, jnp.where(half, b0, b1)], axis=0), diagonal, NN)
        beside = jnp.concatenate([jnp.where(left, 0.0, a0[0:64]), jnp.where(left, a1[64:128], 0.0)], axis=0)
        update = mm_split(solved, beside, NN)
        rest = jnp.where(left, a1[0:64], a0[64:128]) - update[0:64]
        side = jnp.where(half, b1, b0) - update[64:80]
        second = jnp.concatenate(right_divide(rows_of(rest) + rows_of(side))[0:2], axis=0)
        under = solved[0:64]
        back = jnp.concatenate([jnp.where(left, 0.0, under), jnp.where(left, under, 0.0)], axis=0)
        first = solved[64:80] - mm_split(second, back, NN)
        copy(psend.at[remote], parr.at[remote], ORDER[0], psend_sem, precv.at[0]).wait_send()
        copy(fsend.at[remote], farr.at[remote], ORDER[0], fsend_sem, frecv.at[0]).wait_send()
        current[0] = jnp.where(half, first, second)
        current[1] = jnp.where(half, second, first)
        return carry

    lax.fori_loop(0, LAYERS, layer, 0)
    precoders_out[...] = current[...]


def copy_kernel(a_in, b_in, a_out, b_out):
    a_out[...] = a_in[...]
    b_out[...] = b_in[...]


def body(channels, precoders_init, receiver_cells, transmitter_cells, interferers, counts):
    dma = pltpu.SemaphoreType.DMA
    vmem = pl.BlockSpec(memory_space=pltpu.VMEM)
    slots, wide = pltpu.VMEM((DEV, 16, 128), F32), pltpu.VMEM((DEV, 18, 128), F32)
    shapes = (jax.ShapeDtypeStruct((2, 16, 128), F32), jax.ShapeDtypeStruct((2, 256), F32))
    results = pl.pallas_call(
        kernel,
        out_shape=shapes,
        in_specs=[vmem, vmem, vmem, vmem, pl.BlockSpec(memory_space=pl.ANY), vmem],
        out_specs=(vmem, vmem),
        scratch_shapes=[
            pltpu.VMEM((82, 64, 128), F32),
            pltpu.VMEM((82, 128, 128), BF16),
            pltpu.VMEM((2, 16, 128), F32),
            slots, slots, slots, wide, wide,
            pltpu.VMEM((2, 2, 128), F32),
            pltpu.VMEM((2, 32, 128), BF16),
            pltpu.VMEM((128, 256), F32),
            pltpu.VMEM((8, 256), jnp.int32),
            pltpu.SMEM((8, 256), jnp.int32),
            dma, dma, dma, dma((len(GROUPS),)), dma, dma((len(GROUPS),)),
        ],
        compiler_params=pltpu.CompilerParams(collective_id=0, has_side_effects=True),
    )(
        receiver_cells.reshape(1, 256), transmitter_cells.reshape(1, 256), counts.reshape(1, 256), interferers.T,
        channels.reshape(82, 64, 128), precoders_init,
    )
    return pl.pallas_call(copy_kernel, out_shape=shapes, in_specs=[vmem, vmem], out_specs=(vmem, vmem))(*results)


def solution(mesh):
    return jax.shard_map(
        body,
        mesh=mesh,
        in_specs=(P("cells", None, None, None), P("cells", None, None), P(), P(), P(), P()),
        out_specs=(P("cells", None, None), P("cells", None)),
        check_vma=False,
    )
```

```python
import random

import jax
import jax.numpy as jnp
from jax import lax
from jax.experimental import pallas as pl
from jax.experimental.pallas import tpu as pltpu
from jax.sharding import PartitionSpec as P

LAYERS = 4
STEP_SIZES = (0.3, 0.2, 0.15, 0.1)
HIGHEST = lax.Precision.HIGHEST
MESH = pl.DeviceIdType.MESH
F32, BF16 = jnp.float32, jnp.bfloat16
DEV = 128
OFFSETS = [(z, x, y, c) for z in range(4) for x in range(4) for y in range(4) for c in range(2)]
shuffled = random.Random(5)
ORDER = sorted(range(DEV), key=lambda i: (-sum(min(a, 4 - a) for a in OFFSETS[i][:3]), -i if i < 2 else shuffled.random()))
SIZES = [16, 16, 16, 16, 32, 32]
GROUPS = [ORDER[sum(SIZES[:g]) : sum(SIZES[: g + 1])] for g in range(len(SIZES))]
LAST = len(GROUPS) - 1
NN = (((1,), (0,)), ((), ()))
NT = (((1,), (1,)), ((), ()))
TN = (((0,), (0,)), ((), ()))


def split(x):
    high = x.astype(BF16)
    return high, (x - high.astype(F32)).astype(BF16)


def mm(a, b, dims):
    return lax.dot_general(a, b, dims, preferred_element_type=F32)


def mm_exact(a, b, dims):
    return lax.dot_general(a, b, dims, precision=HIGHEST, preferred_element_type=F32)


def mm_split(a, b, dims):
    (ah, al), (bh, bl) = split(a), split(b)
    return mm(ah, bh, dims) + (mm(ah, bl, dims) + mm(al, bh, dims))


def lanes():
    return lax.broadcasted_iota(jnp.int32, (8, 128), 1)


def pick_row(v, row):
    return jnp.broadcast_to(v[row : row + 1, :], (8, 128))


def pick_lane(v, k):
    return jnp.take_along_axis(v, jnp.where(lanes() < 64, k, 64 + k), axis=1)


def rows_of(x):
    return [x[8 * i : 8 * i + 8, :] for i in range(x.shape[0] // 8)]


def clear_block(rows, top, others):
    spot, line = lanes() % 64, lax.broadcasted_iota(jnp.int32, (8, 128), 0)
    columns = [pick_lane(rows[top], 8 * top + j) for j in range(8)]
    unit = (spot == line + 8 * top).astype(F32)
    x = rows[top] - unit
    for j in range(0, 8, 2):
        a, b = columns[j], columns[j + 1]
        p11, p21, p12, p22 = pick_row(a, j), pick_row(a, j + 1), pick_row(b, j), pick_row(b, j + 1)
        inverse = 1.0 / (p11 * p22 - p12 * p21)
        a, b = a - (line == j).astype(F32), b - (line == j + 1).astype(F32)
        one, two = (a * p22 - b * p21) * inverse, (b * p11 - a * p12) * inverse
        for later in range(j + 2, 8):
            column = columns[later]
            columns[later] = column - one * pick_row(column, j) - two * pick_row(column, j + 1)
        x = x - one * pick_row(x, j) - two * pick_row(x, j + 1)
    pivots = [pick_row(x, j) for j in range(8)]
    for i in others:
        t = [pick_lane(rows[i], 8 * top + j) * pivots[j] for j in range(8)]
        rows[i] = rows[i] - (((t[0] + t[1]) + (t[2] + t[3])) + ((t[4] + t[5]) + (t[6] + t[7])))
    rows[top] = unit - x


def right_divide(rows):
    rows = list(rows)
    for top in range(8):
        clear_block(rows, top, range(top + 1, len(rows)))
    return rows[8:]


def invert(rows):
    rows = list(rows)
    for top in range(8):
        clear_block(rows, top, [i for i in range(8) if i != top])
    return jnp.concatenate(rows, axis=0)


def lower_divide(w, v):
    ws, vs = rows_of(w), rows_of(v)
    line = lax.broadcasted_iota(jnp.int32, (8, 128), 0)
    diagonal = [jnp.ones((8, 128), F32), jnp.ones((8, 128), F32)]
    for top in range(2):
        columns = [[pick_lane(ws[i], 8 * top + j) for i in range(top, 2)] for j in range(8)]
        for j in range(8):
            pivot = pick_row(columns[j][0], j)
            inverse = 1.0 / pivot
            factors = [c * inverse for c in columns[j]]
            factors[0] = jnp.where(line > j, factors[0], 0.0)
            diagonal[top] = jnp.where(line == j, pivot, diagonal[top])
            for later in range(j + 1, 8):
                row = pick_row(columns[later][0], j)
                columns[later] = [c - f * row for c, f in zip(columns[later], factors)]
            wrow, vrow = pick_row(ws[top], j), pick_row(vs[top], j)
            for i in range(top, 2):
                ws[i] = ws[i] - factors[i - top] * wrow
                vs[i] = vs[i] - factors[i - top] * vrow
    out_l, out_v = [], []
    for i in range(2):
        scale = 1.0 / jnp.sqrt(diagonal[i])
        keep = (lanes() % 64 >= line + 8 * i) & (lanes() % 64 < 16)
        out_l.append(jnp.where(keep, ws[i] * scale, 0.0))
        out_v.append(vs[i] * scale)
    return out_l, jnp.concatenate(out_v, axis=0)


def pack_rows(top, bottom, s):
    out = []
    for part in (top, bottom):
        part = part if s == 0 else pltpu.roll(part, 64, 1)
        part = pltpu.roll(jnp.where(lanes() < 16, part, 0.0), 0, 1, stride=16, stride_axis=0)
        out.append(jnp.sum(part, axis=0, keepdims=True))
    return out


def make_table(me, receivers, transmitters, counts, interferers):
    lane = lax.broadcasted_iota(jnp.int32, (1, 256), 1)
    listed = interferers
    number = lax.broadcasted_iota(jnp.int32, (40, 256), 0)
    used = number < counts
    link, apart, slots, wanted, served = jnp.zeros((1, 256), jnp.int32), [], [], [], []
    for s in range(2):
        mine = lane == 2 * me + s
        cell = jnp.sum(jnp.where(mine, receivers, 0), axis=1, keepdims=True)
        column = jnp.max(jnp.where(mine & used, listed, -1), axis=1, keepdims=True)
        match = (column == transmitters).astype(jnp.int32)
        own = (cell == transmitters).astype(jnp.int32)
        apart.append(jnp.sum(match, axis=0, keepdims=True))
        link = link + jnp.sum(match * (number + (1 + 41 * s)), axis=0, keepdims=True) + own * (41 * s)
        slots.append(jnp.sum(own * lane, axis=1, keepdims=True))
        if s == 1:
            second = apart[1] + own
        cell = jnp.sum(jnp.where(mine, transmitters, 0), axis=1, keepdims=True)
        own = (cell == receivers).astype(jnp.int32)
        wanted.append(jnp.max((used & (listed == cell)).astype(jnp.int32), axis=0, keepdims=True) + own)
        served.append(jnp.sum(own * lane, axis=1, keepdims=True))
    misc = sum(jnp.where(lane == i, v, 0) for i, v in enumerate(slots + served))
    rows = [link, apart[0], apart[1], wanted[0], wanted[1], second]
    rows = [r + pltpu.roll(r, 255, 1) for r in rows] + [misc, misc]
    return [jnp.clip(r, 0, top) for r, top in zip(rows, (81, 1, 1, 1, 1, 1, 255, 255))]


def kernel(
    receivers, transmitters, counts, interferers, channels, first_precoders, precoders_out, weights_out,
    raw, links, current, psend, parr, gbuf, fsend, farr, lower_rows, pair, acc1, tabv, tab,
    raw_sem, tab_sem, psend_sem, precv, fsend_sem, frecv,
):
    me = lax.axis_index("cells")
    mz, mx, my, mc = me // 32, (me // 8) % 4, (me // 2) % 4, me % 2

    zs = [lax.rem(mz + a, 4) * 32 for a in range(4)]
    xs = [lax.rem(mx + a, 4) * 8 for a in range(4)]
    ys = [lax.rem(my + a, 4) * 2 for a in range(4)]
    cs = [mc, 1 - mc]

    def target(k):
        dz, dx, dy, dc = OFFSETS[k]
        return zs[dz] + xs[dx] + ys[dy] + cs[dc]

    def source(k):
        dz, dx, dy, dc = OFFSETS[k]
        return zs[(4 - dz) % 4] + xs[(4 - dx) % 4] + ys[(4 - dy) % 4] + cs[dc]

    def slot_from(d):
        z, x, y, c = d // 32, (d // 8) % 4, (d // 2) % 4, d % 2
        return (((mz + 4 - z) % 4 * 4 + (mx + 4 - x) % 4) * 4 + (my + 4 - y) % 4) * 2 + (mc + 2 - c) % 2

    def copy(src, dst, i, send, recv):
        return pltpu.make_async_remote_copy(
            src_ref=src, dst_ref=dst, send_sem=send, recv_sem=recv,
            device_id=(target(i),), device_id_type=MESH,
        )

    remote = pl.ds(1, DEV - 1)

    def wait_group(buf, g, send, recv):
        part = buf.at[pl.ds(1, SIZES[g] - (g == LAST))]
        copy(part, part, ORDER[0], send, recv.at[g]).wait_recv()

    fetch = pltpu.make_async_copy(channels, raw, raw_sem)
    fetch.start()
    barrier = pltpu.get_barrier_semaphore()

    for k in ORDER[: DEV - 1]:
        pl.semaphore_signal(barrier, inc=1, device_id=(target(k),), device_id_type=MESH)
    current[...] = first_precoders[...]
    table = make_table(me, receivers[...], transmitters[...], counts[...], interferers[...])
    for i in range(8):
        tabv[i : i + 1, :] = table[i]
    lookup = pltpu.make_async_copy(tabv, tab, tab_sem)
    lookup.start()
    half = lax.broadcasted_iota(jnp.int32, (16, 128), 1) < 64
    left = lax.broadcasted_iota(jnp.int32, (64, 128), 1) < 64

    def prepare(i, carry):
        high, low = split(raw[i])
        links[i, 0:64, :] = high
        links[i, 64:128, :] = low
        return carry

    fetch.wait()
    lax.fori_loop(0, 82, prepare, 0)
    lookup.wait()
    pl.semaphore_wait(barrier, DEV - 1)

    def layer(index, carry):
        for g, members in enumerate(GROUPS):
            for k in members:
                psend[k] = current[tab[4, 2 * target(k)]]
            for k in members:
                if k > 0:
                    copy(psend.at[k], parr.at[k], k, psend_sem, precv.at[g]).start()
        parr[0] = psend[0]

        for g, members in enumerate(GROUPS):
            wait_group(parr, g, psend_sem, precv)
            highs, lows = [], []
            for i in members:
                d = source(i)
                high, low = split(parr[i])
                product = mm(jnp.concatenate([high, low], axis=0), links[tab[0, 2 * d]], NT)
                total = product[0:16] + product[16:32]
                total = total + pltpu.roll(total, 64, 1)
                gbuf[i] = total
                masked = total * jnp.where(half, tab[1, 2 * d].astype(F32), tab[2, 2 * d].astype(F32))
                high, low = split(masked)
                highs.append(high)
                lows.append(low)
            high, low = jnp.concatenate(highs, axis=0), jnp.concatenate(lows, axis=0)
            one = mm(high, high, TN) + (mm(high, low, TN) + mm(low, high, TN))
            acc1[:, 0:128] = one if g == 0 else acc1[:, 0:128] + one

        full = acc1[:, 0:128]
        line = lax.broadcasted_iota(jnp.int32, (64, 128), 0)
        spot = lax.broadcasted_iota(jnp.int32, (64, 128), 1) % 64
        covariance = jnp.where(left, full[0:64], full[64:128]) + (line == spot).astype(F32)
        direct = jnp.where(half, gbuf[slot_from(tab[6, 0] // 2)], gbuf[slot_from(tab[6, 1] // 2)])
        v = jnp.concatenate(right_divide(rows_of(covariance) + rows_of(direct))[0:2], axis=0)
        blank = jnp.zeros((48, 128), F32)
        apart = jnp.concatenate(
            [jnp.where(half, direct, 0.0), blank, jnp.where(half, 0.0, direct), blank], axis=0
        )
        short = lax.broadcasted_iota(jnp.int32, (16, 128), 0)
        w = mm_split(v, apart, NT)
        w = w + (lax.broadcasted_iota(jnp.int32, (16, 128), 1) % 64 == short).astype(F32)
        lower, filters = lower_divide(w, v)
        for s in range(2):
            mine = jnp.where(half, filters, 0.0) if s == 0 else jnp.where(half, 0.0, filters)
            mine = mine + pltpu.roll(mine, 64, 1)
            high, low = split(mine)
            pair[s] = jnp.concatenate([high, low], axis=0)
        for s in range(2):
            for i, row in enumerate(pack_rows(lower[0], lower[1], s)):
                lower_rows[s, i : i + 1, :] = row

        for g, members in enumerate(GROUPS):
            width = 8 if g == 0 else 16
            for batch in [members[i : i + width] for i in range(0, len(members), width)]:
                for k in batch:
                    d = 2 * target(k)
                    product = mm(pair[tab[5, d]], links[tab[0, d]], NN)
                    fsend[k, 0:16, :] = product[0:16] + product[16:32]
                    fsend[k, 16:18, :] = lower_rows[tab[5, d]]
                for k in batch:
                    if k > 0:
                        copy(fsend.at[k], farr.at[k], k, fsend_sem, frecv.at[g]).start()
        farr[0] = fsend[0]
        for s in range(2):
            for i, row in enumerate(pack_rows(w[0:8], w[8:16], s)):
                weights_out[s : s + 1, 128 * i : 128 * i + 128] = row

        for g, members in enumerate(GROUPS):
            wait_group(farr, g, fsend_sem, frecv)
            highs, lows, highs01, lows01 = [], [], [], []
            for i in members:
                d = source(i)
                m0, m1 = tab[3, 2 * d].astype(F32), tab[4, 2 * d].astype(F32)
                f = farr[i, 0:16, :]
                high, low = split(f)
                highs.append(high)
                lows.append(low)
                high, low = split(jnp.concatenate([f * m0, f * m1], axis=1))
                highs01.append(high)
                lows01.append(low)
            high, low = jnp.concatenate(highs, axis=0), jnp.concatenate(lows, axis=0)
            high01, low01 = jnp.concatenate(highs01, axis=0), jnp.concatenate(lows01, axis=0)
            one = mm(high, high01, TN) + (mm(high, low01, TN) + mm(low, high01, TN))
            acc1[...] = one if g == 0 else acc1[...] + one

        mu = jnp.where(index == 0, STEP_SIZES[0], jnp.where(index == 1, STEP_SIZES[1], jnp.where(index == 2, STEP_SIZES[2], STEP_SIZES[3]))).astype(F32)
        eye = (
            lax.broadcasted_iota(jnp.int32, (128, 128), 0) == lax.broadcasted_iota(jnp.int32, (128, 128), 1)
        ).astype(F32) * mu
        a0, a1 = acc1[:, 0:128] + eye, acc1[:, 128:256] + eye
        steps = [slot_from(tab[6, 2 + t] // 2) for t in range(2)]
        low16 = lanes() < 16
        unpack = (lanes() + 16 * lax.broadcasted_iota(jnp.int32, (8, 128), 0)) % 128
        sides = []
        for t in range(2):
            got = farr[steps[t], 16:18, :]
            triangle = jnp.concatenate(
                [
                    jnp.where(low16, jnp.take_along_axis(pick_row(got, i), unpack, axis=1), 0.0)
                    for i in range(2)
                ],
                axis=0,
            )
            sides.append(mm_exact(triangle, farr[steps[t], 0:16, :], TN)[0:16])
        b0, b1 = sides
        upper = jnp.where(left, a0[0:64], a1[64:128])
        under = jnp.where(left, a0[64:128], a1[0:64])
        inverse = invert(rows_of(upper))
        diagonal = jnp.concatenate([jnp.where(left, inverse, 0.0), jnp.where(left, 0.0, inverse)], axis=0)
        solved = mm_split(jnp.concatenate([under, jnp.where(half, b0, b1)], axis=0), diagonal, NN)
        beside = jnp.concatenate([jnp.where(left, 0.0, a0[0:64]), jnp.where(left, a1[64:128], 0.0)], axis=0)
        update = mm_split(solved, beside, NN)
        rest = jnp.where(left, a1[0:64], a0[64:128]) - update[0:64]
        side = jnp.where(half, b1, b0) - update[64:80]
        second = jnp.concatenate(right_divide(rows_of(rest) + rows_of(side))[0:2], axis=0)
        under = solved[0:64]
        back = jnp.concatenate([jnp.where(left, 0.0, under), jnp.where(left, under, 0.0)], axis=0)
        first = solved[64:80] - mm_split(second, back, NN)
        copy(psend.at[remote], parr.at[remote], ORDER[0], psend_sem, precv.at[0]).wait_send()
        copy(fsend.at[remote], farr.at[remote], ORDER[0], fsend_sem, frecv.at[0]).wait_send()
        current[0] = jnp.where(half, first, second)
        current[1] = jnp.where(half, second, first)
        return carry

    lax.fori_loop(0, LAYERS, layer, 0)
    precoders_out[...] = current[...]


def copy_kernel(a_in, b_in, a_out, b_out):
    a_out[...] = a_in[...]
    b_out[...] = b_in[...]


def body(channels, precoders_init, receiver_cells, transmitter_cells, interferers, counts):
    dma = pltpu.SemaphoreType.DMA
    vmem = pl.BlockSpec(memory_space=pltpu.VMEM)
    slots, wide = pltpu.VMEM((DEV, 16, 128), F32), pltpu.VMEM((DEV, 18, 128), F32)
    shapes = (jax.ShapeDtypeStruct((2, 16, 128), F32), jax.ShapeDtypeStruct((2, 256), F32))
    results = pl.pallas_call(
        kernel,
        out_shape=shapes,
        in_specs=[vmem, vmem, vmem, vmem, pl.BlockSpec(memory_space=pl.ANY), vmem],
        out_specs=(vmem, vmem),
        scratch_shapes=[
            pltpu.VMEM((82, 64, 128), F32),
            pltpu.VMEM((82, 128, 128), BF16),
            pltpu.VMEM((2, 16, 128), F32),
            slots, slots, slots, wide, wide,
            pltpu.VMEM((2, 2, 128), F32),
            pltpu.VMEM((2, 32, 128), BF16),
            pltpu.VMEM((128, 256), F32),
            pltpu.VMEM((8, 256), jnp.int32),
            pltpu.SMEM((8, 256), jnp.int32),
            dma, dma, dma, dma((len(GROUPS),)), dma, dma((len(GROUPS),)),
        ],
        compiler_params=pltpu.CompilerParams(collective_id=0, has_side_effects=True),
    )(
        receiver_cells.reshape(1, 256), transmitter_cells.reshape(1, 256), counts.reshape(1, 256), interferers.T,
        channels.reshape(82, 64, 128), precoders_init,
    )
    return pl.pallas_call(copy_kernel, out_shape=shapes, in_specs=[vmem, vmem], out_specs=(vmem, vmem))(*results)


def solution(mesh):
    return jax.shard_map(
        body,
        mesh=mesh,
        in_specs=(P("cells", None, None, None), P("cells", None, None), P(), P(), P(), P()),
        out_specs=(P("cells", None, None), P("cells", None)),
        check_vma=False,
    )
```
